512 devices in a mesh: wide: 128 (over z, y, core), narrow: 4 (over x).
Axes of the slice: x: 4, y: 4, z: 16, core: 2. Of those that a mesh axis runs over, the one named last changes fastest.
Arguments:
- tokens: bfloat16 [1024, 1024], P('wide', 'narrow'), may hold values from -6 to 6
- norm_gain: float32 [1024], replicated, may hold values from 0.1 to 1.9
- w_qk: bfloat16 [1024, 2, 1024], P(None, None, 'narrow'), may hold values from -0.0625 to 0.0625
- w_value: bfloat16 [1024, 1024], P(None, 'narrow'), may hold values from -0.1875 to 0.1875
- w_out: bfloat16 [1024, 1024], P('narrow'), may hold values from -1.5 to 1.5
- kv_cache: bfloat16 [8192, 2, 32, 1024], P('wide', None, None, 'narrow'), may hold values from -200 to 200
- cache_len: int32 [1024], replicated, may hold values from 1 to 256, as said below
- page_table: int32 [1024, 8], replicated, may hold values from 0 to 63, as said below
Outputs:
- attended: bfloat16 [1024, 1024], P('wide', 'narrow')
The draws below stay inside these ranges and needn't reach their ends.
Inputs may be any that keep to these rules, and one draw needn't show every extreme that they name: `cache_len`: every request has one or more cached positions, and some request has exactly 256. `page_table`: on every owner, the pairs (request, page) placed there by the rule of the steps occupy its 64 slots one to one.
All inputs are finite; a program needn't handle non-finite values.
Results may differ from the reference program's by a relative error of at most 0.015.
The reference program's roundings to bfloat16 on the way (of `normed`, `queries`, `pages` and `heads_out`) count: a program that leaves them out, or rounds other values in their place, can miss the bound.
Values may be sent and summed in bfloat16 or wider, within the bound.
A program may use at most 64 MiB of HBM per device.

```python
import jax
import jax.numpy as jnp
from jax import lax

D = 1024
HEADS = 16
HEAD_DIM = 64
TOK_DEV = 8
PAGE = 32
MAXP = 8
TOKENS = 1024
OWNERS = 128
STRIDE = 16


def draw_cache_len(key, part):
    lengths = jax.random.randint(key, (TOKENS,), 1, MAXP * PAGE + 1).astype(jnp.int32)
    return lengths.at[0].set(MAXP * PAGE)


def draw_page_table(key, part):
    slot_count = TOK_DEV * MAXP
    owner_keys = jax.random.split(jax.random.fold_in(key, 7), OWNERS)
    shuffles = jax.vmap(lambda single: jax.random.permutation(single, slot_count))(owner_keys)
    request_ids = jnp.arange(TOKENS, dtype=jnp.int32)[:, None]
    page_ids = jnp.arange(MAXP, dtype=jnp.int32)[None, :]
    offsets = (page_ids - page_ids % 2) * STRIDE + page_ids % 2
    owner = (request_ids // TOK_DEV + offsets) % OWNERS
    within = request_ids % TOK_DEV * MAXP + page_ids
    return shuffles[owner, within].astype(jnp.int32)


def draw_kv_cache(key, part):
    row_count = OWNERS * TOK_DEV * MAXP
    key_base = jax.random.fold_in(key, 11)
    key_value = jax.random.fold_in(key, 12)
    key_offset = jax.random.fold_in(key, 13)
    key_strength = jax.random.fold_in(key, 14)
    key_ratio = jax.random.fold_in(key, 15)
    key_noise = jax.random.fold_in(key, 16)
    base_keys = jnp.clip(0.6 * jax.random.normal(key_base, (row_count, PAGE, D), jnp.float32), -2.4, 2.4)
    base_values = jnp.clip(0.6 * jax.random.normal(key_value, (row_count, PAGE, D), jnp.float32), -2.4, 2.4)
    offset = jax.random.randint(key_offset, (), 0, 32)
    strong_rows = (jnp.arange(row_count, dtype=jnp.int32) + offset) % 32 == 0
    low_log, high_log = (2.5, 3.7)
    strength = jnp.exp(jax.random.uniform(key_strength, (row_count,), jnp.float32, low_log, high_log))
    paired = base_keys.reshape(row_count, PAGE // 2, 2, D)
    even_keys = paired[:, :, 0, :]
    ratio = jax.random.uniform(key_ratio, (row_count, PAGE // 2, 1), jnp.float32, 0.004, 0.012)
    noise = jnp.clip(0.3 * jax.random.normal(key_noise, (row_count, PAGE // 2, D), jnp.float32), -0.9, 0.9)
    odd_keys = even_keys * (1.0 + ratio) + noise
    strong_keys = jnp.stack([even_keys, odd_keys], axis=2).reshape(row_count, PAGE, D) * strength[:, None, None]
    keys_out = jnp.where(strong_rows[:, None, None], strong_keys, base_keys)
    return jnp.stack([keys_out, base_values], axis=1).astype(jnp.bfloat16)


def block_scale(rng, shape, cuts, least, high):
    def one(axis_at, parts):
        steps = jax.random.uniform(jax.random.fold_in(jax.random.fold_in(rng, 6), axis_at), (parts,), jnp.float32, least / len(cuts), high / len(cuts))
        return jnp.repeat(jnp.exp(steps), shape[axis_at] // parts).reshape((-1,) + (1,) * (len(shape) - axis_at - 1))

    factor_of = one(*cuts[0])
    for cut in cuts[1:]:
        factor_of = factor_of * one(*cut)
    return factor_of


def gaussian(key, shape, deviation, bound, shards=(), kind=jnp.bfloat16):
    level = block_scale(key, shape, shards, -0.22, 0.18) if shards else 1.0
    values = jax.random.normal(key, shape, jnp.float32) * deviation * level
    return jnp.minimum(jnp.maximum(values, -bound), bound).astype(kind)


def setup_inputs(seed: int = 0) -> dict:
    key_list = jax.random.split(jax.random.key(seed), 9)
    tokens = gaussian(key_list[0], (TOKENS, D), 1.0, 6.0, ((0, 128), (1, 4)))
    norm_gain = jnp.clip(1.0 + 0.18 * jax.random.normal(key_list[1], (D,), jnp.float32), 0.1, 1.9)
    w_qk = gaussian(key_list[2], (D, 2, D), (8 * D) ** -0.5, 0.0625, ((2, 4),))
    w_value = gaussian(key_list[3], (D, D), D ** -0.5, 0.1875, ((1, 4),))
    w_out = gaussian(key_list[4], (D, D), 0.25, 1.5, ((0, 4),))
    kv_cache = draw_kv_cache(jax.random.fold_in(key_list[8], 71), 0)
    cache_len = draw_cache_len(jax.random.fold_in(key_list[8], 71), 0)
    page_table = draw_page_table(jax.random.fold_in(key_list[8], 71), 0)
    return {"tokens": tokens, "norm_gain": norm_gain, "w_qk": w_qk, "w_value": w_value, "w_out": w_out, "kv_cache": kv_cache, "cache_len": cache_len, "page_table": page_table}


def reference(tokens, norm_gain, w_qk, w_value, w_out, kv_cache, cache_len, page_table):
    floats = tokens.astype(jnp.float32)
    normed = (floats * lax.rsqrt(lax.optimization_barrier(jnp.mean(floats * floats, axis=-1, keepdims=True)) + 1e-06) * norm_gain).astype(jnp.bfloat16)
    both = jnp.einsum('td,dcf->tcf', normed.astype(jnp.float32), w_qk.astype(jnp.float32)).astype(jnp.bfloat16)
    queries = both[:, 0, :]
    new_keys = both[:, 1, :]
    new_values = jnp.dot(normed, w_value, preferred_element_type=jnp.float32).astype(jnp.bfloat16)
    slot_count = TOK_DEV * MAXP
    request_ids = jnp.arange(TOKENS, dtype=jnp.int32)
    page_ids = jnp.arange(MAXP, dtype=jnp.int32)
    offsets = (page_ids - page_ids % 2) * STRIDE + page_ids % 2
    owner = (request_ids[:, None] // TOK_DEV + offsets[None, :]) % OWNERS
    rows_all = (owner * slot_count + page_table).astype(jnp.int32)
    positions = page_ids[:, None] * PAGE + jnp.arange(PAGE, dtype=jnp.int32)[None, :]

    def one_block(block):
        q_block, k_block, v_block, rows, lengths = block
        count = q_block.shape[0]
        pages = kv_cache[rows]
        keys = pages[:, :, 0].reshape(count, MAXP, PAGE, HEADS, HEAD_DIM).astype(jnp.float32)
        values = pages[:, :, 1].reshape(count, MAXP, PAGE, HEADS, HEAD_DIM).astype(jnp.float32)
        q_heads = q_block.reshape(count, HEADS, HEAD_DIM).astype(jnp.float32)
        scores = jnp.einsum('bhe,bjphe->bjhp', q_heads, keys)
        valid = (positions[None, :, :] < lengths[:, None, None])[:, :, None, :]
        scores = jnp.where(valid, scores, -1e+30)
        page_max = lax.optimization_barrier(jnp.max(scores, axis=-1))
        weights = jnp.where(valid, jnp.exp(scores - page_max[..., None]), 0.0)
        page_sum = lax.optimization_barrier(jnp.sum(weights, axis=-1))
        rounded = lax.optimization_barrier(weights.astype(jnp.bfloat16)).astype(jnp.float32)
        page_acc = jnp.einsum('bjhp,bjphe->bjhe', rounded, values)
        self_score = lax.optimization_barrier(jnp.sum(q_heads * k_block.reshape(count, HEADS, HEAD_DIM).astype(jnp.float32), axis=-1))
        top = jnp.maximum(lax.optimization_barrier(jnp.max(page_max, axis=1)), self_score)
        factor = jnp.exp(page_max - top[:, None, :])
        self_factor = jnp.exp(self_score - top)
        numer = lax.optimization_barrier(jnp.sum(factor[..., None] * page_acc, axis=1)) + self_factor[..., None] * v_block.reshape(count, HEADS, HEAD_DIM).astype(jnp.float32)
        denom = lax.optimization_barrier(jnp.sum(factor * page_sum, axis=1)) + self_factor
        return (numer / denom[..., None]).reshape(count, D).astype(jnp.bfloat16)
    blocks = TOKENS // TOK_DEV
    heads_out = lax.map(one_block, (queries.reshape(blocks, TOK_DEV, D), new_keys.reshape(blocks, TOK_DEV, D), new_values.reshape(blocks, TOK_DEV, D), rows_all.reshape(blocks, TOK_DEV, MAXP), cache_len.reshape(blocks, TOK_DEV)))
    heads_out = heads_out.reshape(TOKENS, D)
    return jnp.dot(heads_out, w_out, preferred_element_type=jnp.float32).astype(jnp.bfloat16)
```

```python
import functools

import jax
import jax.numpy as jnp
from jax import lax
from jax.experimental import pallas as pl
from jax.experimental.pallas import tpu as pltpu
from jax.sharding import PartitionSpec as P

HEAD_DIM = 64
MESH = pl.DeviceIdType.MESH
NEG = -1e30


def layer_kernel(
    wide, narrow, offs,
    tok, gain, wqk, wv, wo, kv, clen, ptab, out,
    tokb, gainb, wqkb, wvb, wob, kvb, lenb, ptb, qin, pout, pin, rsout, rsin,
    lsem, tsend, trecv, qsend, qrecv, psend, precv, rsend, rrecv,
):
    me_w = lax.axis_index("wide")
    me_x = lax.axis_index("narrow")
    tcount, width = tok.shape
    pages = len(offs)
    heads = width // HEAD_DIM
    page_len = kvb.shape[2]
    span = tcount * page_len

    def fwd(j):
        return lax.rem(me_w + offs[j], wide)

    def bwd(j):
        return lax.rem(me_w + (wide - offs[j]), wide)

    local = [
        pltpu.make_async_copy(tok, tokb.at[me_x], lsem.at[0]),
        pltpu.make_async_copy(gain, gainb, lsem.at[1]),
        pltpu.make_async_copy(wqk, wqkb, lsem.at[2]),
        pltpu.make_async_copy(wv, wvb, lsem.at[3]),
        pltpu.make_async_copy(clen, lenb, lsem.at[4]),
        pltpu.make_async_copy(ptab, ptb, lsem.at[5]),
        pltpu.make_async_copy(kv, kvb, lsem.at[6]),
        pltpu.make_async_copy(wo, wob, lsem.at[7]),
    ]
    for copy in local:
        copy.start()

    around = sorted({o for o in offs if o} | {wide - o for o in offs if o})
    barrier = pltpu.get_barrier_semaphore()
    for d in range(1, narrow):
        pl.semaphore_signal(
            barrier, inc=1, device_id=(me_w, lax.rem(me_x + d, narrow)), device_id_type=MESH
        )
    for o in around:
        pl.semaphore_signal(
            barrier, inc=1, device_id=(lax.rem(me_w + o, wide), me_x), device_id_type=MESH
        )
    pl.semaphore_wait(barrier, narrow - 1 + len(around))

    tcopies = [
        pltpu.make_async_remote_copy(
            src_ref=tok, dst_ref=tokb.at[me_x], send_sem=tsend.at[d - 1], recv_sem=trecv.at[d - 1],
            device_id=(me_w, lax.rem(me_x + d, narrow)), device_id_type=MESH,
        )
        for d in range(1, narrow)
    ]
    for copy in tcopies:
        copy.start()
    local[0].wait()
    local[1].wait()
    for copy in tcopies:
        copy.wait_recv()

    floats = [tokb[i].astype(jnp.float32) for i in range(narrow)]
    square = functools.reduce(
        jnp.add, [jnp.sum(f * f, axis=-1, keepdims=True) for f in floats]
    )
    scale = lax.rsqrt(square / (narrow * width) + 1e-06)
    normed = [
        (floats[i] * scale * gainb[:, i * width:(i + 1) * width]).astype(jnp.bfloat16)
        for i in range(narrow)
    ]

    local[2].wait()

    def project(weight):
        return functools.reduce(
            jnp.add,
            [
                jnp.dot(
                    normed[i], weight(i * width, (i + 1) * width),
                    preferred_element_type=jnp.float32,
                )
                for i in range(narrow)
            ],
        ).astype(jnp.bfloat16)

    query = project(lambda a, b: wqkb[a:b, 0, :])
    qin[0] = query
    qcopies = {
        j: pltpu.make_async_remote_copy(
            src_ref=qin.at[0], dst_ref=qin.at[j], send_sem=qsend.at[j], recv_sem=qrecv.at[j],
            device_id=(fwd(j), me_x), device_id_type=MESH,
        )
        for j in range(1, pages)
    }
    far = sorted(range(1, pages), key=lambda j: -min(offs[j], wide - offs[j]))
    for j in far:
        qcopies[j].start()

    new_keys = project(lambda a, b: wqkb[a:b, 1, :]).astype(jnp.float32)
    local[3].wait()
    new_values = project(lambda a, b: wvb[a:b, :]).astype(jnp.float32)
    products = query.astype(jnp.float32) * new_keys
    lane = lax.broadcasted_iota(jnp.int32, (tcount, 128), 1)
    head_of = lax.broadcasted_iota(jnp.int32, (tcount, width), 1) // HEAD_DIM

    def stat_tile(columns, base, start):
        tile = start
        for h, column in enumerate(columns):
            tile = jnp.where(lane == base + h, column, tile)
        return tile

    self_score = stat_tile(
        [
            jnp.sum(jnp.where(head_of == h, products, 0.0), axis=-1, keepdims=True)
            for h in range(heads)
        ],
        0, jnp.full((tcount, 128), NEG, jnp.float32),
    )

    local[4].wait()
    local[5].wait()
    local[6].wait()
    row = lax.broadcasted_iota(jnp.int32, (tcount, span), 0)
    place = lax.broadcasted_iota(jnp.int32, (tcount, span), 1) - row * page_len

    def attend(j):
        home = bwd(j) * tcount
        q = qin[j].astype(jnp.float32)
        spread = jnp.concatenate(
            [jnp.where(head_of == h, q, 0.0) for h in range(heads)], axis=0
        ).astype(jnp.bfloat16)
        slots = [ptb[j, home + r] for r in range(tcount)]
        keys = jnp.concatenate([kvb[s, 0] for s in slots], axis=0)
        values = jnp.concatenate([kvb[s, 1] for s in slots], axis=0)
        limit = jnp.full((tcount, span), 0, jnp.int32)
        for r in range(tcount):
            limit = jnp.where(
                row == r, jnp.minimum(lenb[home + r] - j * page_len, page_len), limit
            )
        valid1 = (place >= 0) & (place < limit)
        valid = jnp.concatenate([valid1] * heads, axis=0)
        scores = lax.dot_general(
            spread, keys, (((1,), (1,)), ((), ())), preferred_element_type=jnp.float32
        )
        scores = jnp.where(valid, scores, NEG)
        top = jnp.max(scores, axis=-1, keepdims=True)
        weights = jnp.where(valid, jnp.exp(scores - top), 0.0)
        total = jnp.sum(weights, axis=-1, keepdims=True)
        acc = jnp.dot(weights.astype(jnp.bfloat16), values, preferred_element_type=jnp.float32)
        mine = jnp.zeros((tcount, width), jnp.float32)
        for h in range(heads):
            mine = jnp.where(head_of == h, acc[h * tcount:(h + 1) * tcount], mine)
        stats = stat_tile(
            [top[h * tcount:(h + 1) * tcount] for h in range(heads)],
            0, jnp.full((tcount, 128), 0.0, jnp.float32),
        )
        stats = stat_tile(
            [total[h * tcount:(h + 1) * tcount] for h in range(heads)], 64, stats
        )
        return mine, stats

    pcopies = {
        j: pltpu.make_async_remote_copy(
            src_ref=pout.at[j], dst_ref=pin.at[j], send_sem=psend.at[j], recv_sem=precv.at[j],
            device_id=(bwd(j), me_x), device_id_type=MESH,
        )
        for j in range(1, pages)
    }
    mine, stats = attend(0)
    pin[0, :, :width] = mine
    pin[0, :, width:] = stats
    for j in reversed(far):
        qcopies[j].wait_recv()
        mine, stats = attend(j)
        pout[j, :, :width] = mine
        pout[j, :, width:] = stats
        pcopies[j].start()

    for j in reversed(far):
        pcopies[j].wait_recv()

    stats = [pin[j, :, width:] for j in range(pages)]
    best = functools.reduce(jnp.maximum, stats, self_score)
    self_factor = jnp.exp(self_score - best)
    factors = [jnp.exp(s - best) for s in stats]
    denom = self_factor
    for j in range(pages):
        denom = denom + factors[j] * pltpu.roll(stats[j], 64, 1)

    def widen(tile):
        wide_tile = jnp.zeros((tcount, width), jnp.float32)
        for h in range(heads):
            wide_tile = jnp.where(head_of == h, tile[:, h:h + 1], wide_tile)
        return wide_tile

    numer = widen(self_factor) * new_values
    for j in range(pages):
        numer = numer + widen(factors[j]) * pin[j, :, :width]
    heads_out = (numer / widen(denom)).astype(jnp.bfloat16)

    local[7].wait()
    rcopies = []
    for d in range(1, narrow):
        peer = lax.rem(me_x + d, narrow)
        start = pl.multiple_of(peer * width, width)
        rsout[d - 1] = jnp.dot(
            heads_out, wob[:, pl.ds(start, width)], preferred_element_type=jnp.float32
        )
        copy = pltpu.make_async_remote_copy(
            src_ref=rsout.at[d - 1], dst_ref=rsin.at[d - 1],
            send_sem=rsend.at[d - 1], recv_sem=rrecv.at[d - 1],
            device_id=(me_w, peer), device_id_type=MESH,
        )
        copy.start()
        rcopies.append(copy)
    start = pl.multiple_of(me_x * width, width)
    total = jnp.dot(heads_out, wob[:, pl.ds(start, width)], preferred_element_type=jnp.float32)
    for d in range(1, narrow):
        rcopies[d - 1].wait_recv()
        total = total + rsin[d - 1]
    out[...] = total.astype(out.dtype)
    for copy in tcopies + rcopies + [qcopies[j] for j in far] + [pcopies[j] for j in far]:
        copy.wait_send()


def body(wide, narrow, tokens, norm_gain, w_qk, w_value, w_out, kv_cache, cache_len, page_table):
    tcount, width = tokens.shape
    total, pages = page_table.shape
    features = norm_gain.shape[0]
    stride_len = wide // pages
    offs = tuple(((j - j % 2) * stride_len + j % 2) % wide for j in range(pages))
    anywhere = pl.BlockSpec(memory_space=pl.ANY)
    dma = pltpu.SemaphoreType.DMA
    return pl.pallas_call(
        functools.partial(layer_kernel, wide, narrow, offs),
        out_shape=jax.ShapeDtypeStruct((tcount, width), jnp.bfloat16),
        in_specs=[anywhere] * 8,
        out_specs=pl.BlockSpec(memory_space=pltpu.VMEM),
        scratch_shapes=[
            pltpu.VMEM((narrow, tcount, width), jnp.bfloat16),
            pltpu.VMEM((1, features), jnp.float32),
            pltpu.VMEM(w_qk.shape, jnp.bfloat16),
            pltpu.VMEM(w_value.shape, jnp.bfloat16),
            pltpu.VMEM(w_out.shape, jnp.bfloat16),
            pltpu.VMEM(kv_cache.shape, jnp.bfloat16),
            pltpu.SMEM((total,), jnp.int32),
            pltpu.SMEM((pages, total), jnp.int32),
            pltpu.VMEM((pages, tcount, width), jnp.bfloat16),
            pltpu.VMEM((pages, tcount, width + 128), jnp.float32),
            pltpu.VMEM((pages, tcount, width + 128), jnp.float32),
            pltpu.VMEM((narrow - 1, tcount, width), jnp.float32),
            pltpu.VMEM((narrow - 1, tcount, width), jnp.float32),
            dma((8,)),
            dma((narrow - 1,)), dma((narrow - 1,)),
            dma((pages,)), dma((pages,)),
            dma((pages,)), dma((pages,)),
            dma((narrow - 1,)), dma((narrow - 1,)),
        ],
        compiler_params=pltpu.CompilerParams(
            collective_id=0, has_side_effects=True, vmem_limit_bytes=62 << 20
        ),
    )(
        tokens, norm_gain.reshape(1, features), w_qk, w_value, w_out, kv_cache, cache_len,
        page_table.T,
    )


def solution(mesh):
    placed = (
        P("wide", "narrow"),
        P(),
        P(None, None, "narrow"),
        P(None, "narrow"),
        P("narrow", None),
        P("wide", None, None, "narrow"),
        P(),
        P(),
    )
    return jax.shard_map(
        functools.partial(body, mesh.shape["wide"], mesh.shape["narrow"]),
        mesh=mesh, in_specs=placed, out_specs=P("wide", "narrow"), check_vma=False,
    )
```

```python
import functools

import jax
import jax.numpy as jnp
from jax import lax
from jax.experimental import pallas as pl
from jax.experimental.pallas import tpu as pltpu
from jax.sharding import PartitionSpec as P

HEAD_DIM = 64
MESH = pl.DeviceIdType.MESH
NEG = -1e30


def layer_kernel(
    wide, narrow, stride_len,
    tok, gain, wqk, wv, wo, kv, clen, ptab, out,
    tokb, gainb, wqkb, wvb, wob, kvb, lenb, ptb, qin, pout, pin, rsout, rsin,
    lsem, tsend, trecv, qsend, qrecv, psend, precv, rsend, rrecv, esem,
):
    me_w = lax.axis_index("wide")
    me_x = lax.axis_index("narrow")
    tcount, width = tok.shape
    pages = ptab.shape[0]
    offs = tuple((j - j % 2) * stride_len + j % 2 for j in range(pages))
    direct, relayed, answer_order = (1, 2, 3, 6, 7), (4, 5), (2, 3, 6, 7, 1)
    heads = width // HEAD_DIM
    page_len = kvb.shape[2]
    span = tcount * page_len

    local = [
        pltpu.make_async_copy(tok, tokb.at[me_x], lsem.at[0]),
        pltpu.make_async_copy(gain, gainb, lsem.at[1]),
        pltpu.make_async_copy(wqk, wqkb, lsem.at[2]),
        pltpu.make_async_copy(wv, wvb, lsem.at[3]),
        pltpu.make_async_copy(clen, lenb, lsem.at[4]),
        pltpu.make_async_copy(ptab, ptb, lsem.at[5]),
        pltpu.make_async_copy(kv, kvb, lsem.at[6]),
        pltpu.make_async_copy(wo, wob, lsem.at[7]),
    ]

    barrier = pltpu.get_barrier_semaphore()

    def greet(target):
        pl.semaphore_signal(barrier, inc=1, device_id=target, device_id_type=MESH)

    expected = narrow - 1
    for d in range(1, narrow):
        greet((me_w, lax.rem(me_x + d, narrow)))
    for j in direct:
        pl.when(me_w + offs[j] < wide)(lambda j=j: greet((me_w + offs[j], me_x)))
        pl.when(me_w < offs[j])(lambda j=j: greet((me_w + wide - offs[j], me_x)))
        expected = expected + (me_w + wide - offs[j]) // wide + (me_w + offs[j]) // wide
    for j in relayed:
        pl.when(me_w < offs[j])(lambda j=j: greet((me_w + wide - offs[j], me_x)))
        expected = expected + (me_w + offs[j]) // wide
    for copy in local:
        copy.start()
    pl.semaphore_wait(barrier, expected)
    for j in answer_order:
        pl.when(me_w >= offs[j])(
            lambda j=j: pl.semaphore_signal(
                esem.at[j], inc=1, device_id=(me_w - offs[j], me_x), device_id_type=MESH
            )
        )
    tcopies = [
        pltpu.make_async_remote_copy(
            src_ref=tok, dst_ref=tokb.at[me_x], send_sem=tsend.at[d - 1], recv_sem=trecv.at[d - 1],
            device_id=(me_w, lax.rem(me_x + d, narrow)), device_id_type=MESH,
        )
        for d in range(1, narrow)
    ]
    for d in range(1, narrow):
        tcopies[d - 1].start()
    local[0].wait()
    local[1].wait()
    for copy in tcopies:
        copy.wait_recv()

    floats = [tokb[i].astype(jnp.float32) for i in range(narrow)]
    square = functools.reduce(
        jnp.add, [jnp.sum(f * f, axis=-1, keepdims=True) for f in floats]
    )
    scale = lax.rsqrt(square / (narrow * width) + 1e-06)
    normed = [
        (floats[i] * scale * gainb[:, i * width:(i + 1) * width]).astype(jnp.bfloat16)
        for i in range(narrow)
    ]

    local[2].wait()

    def project(weight):
        return functools.reduce(
            jnp.add,
            [
                jnp.dot(
                    normed[i], weight(i * width, (i + 1) * width),
                    preferred_element_type=jnp.float32,
                )
                for i in range(narrow)
            ],
        ).astype(jnp.bfloat16)

    query = project(lambda a, b: wqkb[a:b, 0, :])
    qin[0] = query

    def query_copy(source, o, j):
        return pltpu.make_async_remote_copy(
            src_ref=qin.at[source], dst_ref=qin.at[j], send_sem=qsend.at[j], recv_sem=qrecv.at[j],
            device_id=(lax.rem(me_w + o, wide), me_x), device_id_type=MESH,
        )

    qcopies = {j: query_copy(0, offs[j], j) for j in direct + relayed}
    relays = {j: query_copy(2, offs[j] - offs[2], j) for j in relayed}

    def known(j):
        pl.when(me_w + offs[j] >= wide)(qcopies[j].start)

    def unknown(j):
        @pl.when(me_w + offs[j] < wide)
        def _():
            pl.semaphore_wait(esem.at[j], 1)
            qcopies[j].start()

    for j in relayed + direct:
        known(j)
    for j in (1, 2, 3):
        unknown(j)

    lane = lax.broadcasted_iota(jnp.int32, (tcount, 128), 1)
    head_of = lax.broadcasted_iota(jnp.int32, (tcount, width), 1) // HEAD_DIM

    def stat_tile(columns, base, start):
        tile = start
        for h, column in enumerate(columns):
            tile = jnp.where(lane == base + h, column, tile)
        return tile

    local[4].wait()
    local[5].wait()
    local[6].wait()
    row = lax.broadcasted_iota(jnp.int32, (tcount, span), 0)
    place = lax.broadcasted_iota(jnp.int32, (tcount, span), 1) - row * page_len

    def offset(j):
        return (j - j % 2) * stride_len + j % 2

    def attend(j):
        home = lax.rem(me_w + (wide - offset(j)), wide) * tcount
        q = qin[j].astype(jnp.float32)
        spread = jnp.concatenate(
            [jnp.where(head_of == h, q, 0.0) for h in range(heads)], axis=0
        ).astype(jnp.bfloat16)
        slots = [ptb[j, home + r] for r in range(tcount)]
        keys = jnp.concatenate([kvb[s, 0] for s in slots], axis=0)
        values = jnp.concatenate([kvb[s, 1] for s in slots], axis=0)
        limit = jnp.full((tcount, span), 0, jnp.int32)
        for r in range(tcount):
            limit = jnp.where(
                row == r, jnp.minimum(lenb[home + r] - j * page_len, page_len), limit
            )
        valid1 = (place >= 0) & (place < limit)
        valid = jnp.concatenate([valid1] * heads, axis=0)
        scores = lax.dot_general(
            spread, keys, (((1,), (1,)), ((), ())), preferred_element_type=jnp.float32
        )
        scores = jnp.where(valid, scores, NEG)
        top = jnp.max(scores, axis=-1, keepdims=True)
        weights = jnp.where(valid, jnp.exp(scores - top), 0.0)
        total = jnp.sum(weights, axis=-1, keepdims=True)
        acc = jnp.dot(weights.astype(jnp.bfloat16), values, preferred_element_type=jnp.float32)
        mine = jnp.zeros((tcount, width), jnp.float32)
        for h in range(heads):
            mine = jnp.where(head_of == h, acc[h * tcount:(h + 1) * tcount], mine)
        stats = stat_tile(
            [top[h * tcount:(h + 1) * tcount] for h in range(heads)],
            0, jnp.full((tcount, 128), 0.0, jnp.float32),
        )
        stats = stat_tile(
            [total[h * tcount:(h + 1) * tcount] for h in range(heads)], 64, stats
        )
        return mine, stats

    def partial_copy(j):
        return pltpu.make_async_remote_copy(
            src_ref=pout.at[j], dst_ref=pin.at[j], send_sem=psend.at[j], recv_sem=precv.at[j],
            device_id=(lax.rem(me_w + (wide - offset(j)), wide), me_x), device_id_type=MESH,
        )

    def keep(ref, j, result):
        ref[j, :, :width] = result[0]
        ref[j, :, width:] = result[1]

    for j in direct[3:]:
        unknown(j)

    first = (wide - me_w) // wide

    def turn_of(turn, part):
        return (turn + 3) // 4 * (1 + ((turn + 2) * (1 + part % 2) + 2 * ((3 - part) // 3)) % 3)

    def pair(step, carry):
        turn = (step + first) % 4
        even = 2 * turn_of(turn, me_w * 4 // wide)
        odd = 2 * turn_of(turn, (me_w + first - 1) * 4 // wide) + 1

        @pl.when(turn == 0)
        def _():
            qcopies[1].wait_recv()
            keep(pout, 1, attend(1))
            partial_copy(1).start()

        @pl.when(turn > 0)
        def _():
            query_copy(0, offs[2], even).wait_recv()
            for j in relayed:
                pl.when((even == 2) & (me_w >= offs[2]) & (me_w < wide + offs[2] - offs[j]))(
                    relays[j].start
                )
            query_copy(0, offs[2], odd).wait_recv()
            results = attend(even), attend(odd)
            keep(pout, even, results[0])
            partial_copy(even).start()
            keep(pout, odd, results[1])
            partial_copy(odd).start()

        return carry

    lax.fori_loop(0, pages // 2, pair, 0)
    keep(pin, 0, attend(0))
    new_keys = project(lambda a, b: wqkb[a:b, 1, :]).astype(jnp.float32)
    local[3].wait()
    new_values = project(lambda a, b: wvb[a:b, :]).astype(jnp.float32)
    products = query.astype(jnp.float32) * new_keys
    self_score = stat_tile(
        [
            jnp.sum(jnp.where(head_of == h, products, 0.0), axis=-1, keepdims=True)
            for h in range(heads)
        ],
        0, jnp.full((tcount, 128), NEG, jnp.float32),
    )
    for j in range(1, pages):
        partial_copy(j).wait_recv()

    stats = [pin[j, :, width:] for j in range(pages)]
    best = functools.reduce(jnp.maximum, stats, self_score)
    self_factor = jnp.exp(self_score - best)
    factors = [jnp.exp(s - best) for s in stats]
    denom = self_factor
    for j in range(pages):
        denom = denom + factors[j] * pltpu.roll(stats[j], 64, 1)

    def widen(tile):
        wide_tile = jnp.zeros((tcount, width), jnp.float32)
        for h in range(heads):
            wide_tile = jnp.where(head_of == h, tile[:, h:h + 1], wide_tile)
        return wide_tile

    numer = widen(self_factor) * new_values
    for j in range(pages):
        numer = numer + widen(factors[j]) * pin[j, :, :width]
    heads_out = (numer / widen(denom)).astype(jnp.bfloat16)

    local[7].wait()
    rcopies = []
    for d in range(1, narrow):
        peer = lax.rem(me_x + d, narrow)
        start = pl.multiple_of(peer * width, width)
        rsout[d - 1] = jnp.dot(
            heads_out, wob[:, pl.ds(start, width)], preferred_element_type=jnp.float32
        )
        copy = pltpu.make_async_remote_copy(
            src_ref=rsout.at[d - 1], dst_ref=rsin.at[d - 1],
            send_sem=rsend.at[d - 1], recv_sem=rrecv.at[d - 1],
            device_id=(me_w, peer), device_id_type=MESH,
        )
        copy.start()
        rcopies.append(copy)
    start = pl.multiple_of(me_x * width, width)
    total = jnp.dot(heads_out, wob[:, pl.ds(start, width)], preferred_element_type=jnp.float32)
    for d in range(1, narrow):
        rcopies[d - 1].wait_recv()
        total = total + rsin[d - 1]
    out[...] = total.astype(out.dtype)
    for copy in tcopies + rcopies + [partial_copy(j) for j in range(1, pages)]:
        copy.wait_send()
    for j in direct:
        qcopies[j].wait_send()
    for j in relayed:
        pl.when(me_w + offs[j] >= wide)(qcopies[j].wait_send)
        pl.when((me_w >= offs[2]) & (me_w < wide + offs[2] - offs[j]))(relays[j].wait_send)


def body(wide, narrow, tokens, norm_gain, w_qk, w_value, w_out, kv_cache, cache_len, page_table):
    tcount, width = tokens.shape
    total, pages = page_table.shape
    features = norm_gain.shape[0]
    stride_len = wide // pages
    anywhere = pl.BlockSpec(memory_space=pltpu.HBM)
    dma = pltpu.SemaphoreType.DMA
    return pl.pallas_call(
        functools.partial(layer_kernel, wide, narrow, stride_len),
        out_shape=jax.ShapeDtypeStruct((tcount, width), jnp.bfloat16),
        in_specs=[anywhere] * 8,
        out_specs=pl.BlockSpec(memory_space=pltpu.VMEM),
        scratch_shapes=[
            pltpu.VMEM((narrow, tcount, width), jnp.bfloat16),
            pltpu.VMEM((1, features), jnp.float32),
            pltpu.VMEM(w_qk.shape, jnp.bfloat16),
            pltpu.VMEM(w_value.shape, jnp.bfloat16),
            pltpu.VMEM(w_out.shape, jnp.bfloat16),
            pltpu.VMEM(kv_cache.shape, jnp.bfloat16),
            pltpu.SMEM((total,), jnp.int32),
            pltpu.SMEM((pages, total), jnp.int32),
            pltpu.VMEM((pages, tcount, width), jnp.bfloat16),
            pltpu.VMEM((pages, tcount, width + 128), jnp.float32),
            pltpu.VMEM((pages, tcount, width + 128), jnp.float32),
            pltpu.VMEM((narrow - 1, tcount, width), jnp.float32),
            pltpu.VMEM((narrow - 1, tcount, width), jnp.float32),
            dma((8,)),
            dma((narrow - 1,)), dma((narrow - 1,)),
            dma((pages,)), dma((pages,)),
            dma((pages,)), dma((pages,)),
            dma((narrow - 1,)), dma((narrow - 1,)),
            pltpu.SemaphoreType.REGULAR((pages,)),
        ],
        compiler_params=pltpu.CompilerParams(
            collective_id=0, has_side_effects=True, vmem_limit_bytes=62 << 20
        ),
    )(
        tokens, norm_gain.reshape(1, features), w_qk, w_value, w_out, kv_cache, cache_len,
        page_table.T,
    )


def solution(mesh):
    placed = (
        P("wide", "narrow"),
        P(),
        P(None, None, "narrow"),
        P(None, "narrow"),
        P("narrow", None),
        P("wide", None, None, "narrow"),
        P(),
        P(),
    )
    return jax.shard_map(
        functools.partial(body, mesh.shape["wide"], mesh.shape["narrow"]),
        mesh=mesh, in_specs=placed, out_specs=P("wide", "narrow"), check_vma=False,
    )
```

```python
import functools

import jax
import jax.numpy as jnp
from jax import lax
from jax.experimental import pallas as pl
from jax.experimental.pallas import tpu as pltpu
from jax.sharding import PartitionSpec as P

HEAD_DIM = 64
MESH = pl.DeviceIdType.MESH
ORDERS = (
    ((1, 6, 7, 2, 3, 4, 5), (1, 6, 7, 2, 3, 4, 5), (6, 7, 2, 3, 4, 5, 1)),
    ((1, 2, 3, 6, 7, 4, 5), (1, 2, 3, 6, 7, 4, 5), (1, 2, 7, 6, 3, 4, 5)),
    ((4, 5, 1, 2, 3, 6, 7), (4, 2, 1, 5, 3, 6, 7), (4, 2, 3, 1, 7, 6, 5)),
    ((1, 2, 3, 6, 7, 4, 5), (2, 6, 1, 3, 7, 4, 5), (2, 6, 4, 3, 5, 1, 7)),
)
NEG = -1e30


def layer_kernel(
    wide, narrow, stride_len, row_len,
    tok, gain, wqk, wv, wo, kv, clen, ptab, out,
    tokb, gainb, wqkb, wqb, wvb, wob, kvb, lenb, ptb, qin, pout, pin, rsout, rsin,
    lsem, tsend, trecv, qsend, qrecv, psend, precv, rsend, rrecv, esem, outb,
):
    me_w = lax.axis_index("wide")
    me_x = lax.axis_index("narrow")
    tcount, width = tok.shape
    pages = ptab.shape[0]
    offs = tuple((j - j % 2) * stride_len + j % 2 for j in range(pages))
    direct, relayed, answer_order = (1, 2, 3, 6, 7), (4, 5), (2, 3, 6, 7, 1)
    heads = width // HEAD_DIM
    page_len = kvb.shape[2]
    span = tcount * page_len

    local = [
        pltpu.make_async_copy(tok, tokb.at[me_x], lsem.at[0]),
        pltpu.make_async_copy(gain, gainb, lsem.at[1]),
        pltpu.make_async_copy(wqk, wqkb, lsem.at[2]),
        pltpu.make_async_copy(wv, wvb, lsem.at[3]),
        pltpu.make_async_copy(clen, lenb, lsem.at[4]),
        pltpu.make_async_copy(ptab, ptb, lsem.at[5]),
        pltpu.make_async_copy(kv, kvb, lsem.at[6]),
        pltpu.make_async_copy(wo, wob, lsem.at[7]),
    ]

    barrier = pltpu.get_barrier_semaphore()

    def greet(target):
        pl.semaphore_signal(barrier, inc=1, device_id=target, device_id_type=MESH)

    expected = narrow - 1
    for d in range(1, narrow):
        greet((me_w, lax.rem(me_x + d, narrow)))
    for j in direct[1:]:
        pl.when(me_w + offs[j] < wide)(lambda j=j: greet((me_w + offs[j], me_x)))
        pl.when(me_w < offs[j])(lambda j=j: greet((me_w + wide - offs[j], me_x)))
        expected = expected + (me_w + wide - offs[j]) // wide + (me_w + offs[j]) // wide
    for j in relayed:
        pl.when(me_w < offs[j])(lambda j=j: greet((me_w + wide - offs[j], me_x)))
        expected = expected + (me_w + offs[j]) // wide
    ahead, behind = lax.rem(me_w + 1, wide), lax.rem(me_w + wide - 1, wide)
    in_row = lax.rem(me_w, row_len)
    led = in_row // (row_len - 1) * (me_w // (wide // 2))
    leads = (1 - (in_row + row_len - 1) // row_len) * (behind // (wide // 2))
    pl.when(led == 0)(lambda: greet((ahead, me_x)))
    pl.when(leads == 1)(lambda: greet((behind, me_x)))
    expected = expected + 1 - leads + led
    for copy in local:
        copy.start()
    pl.semaphore_wait(barrier, expected)
    for j in answer_order:
        pl.when(me_w >= offs[j] if j > 1 else leads == 0)(
            lambda j=j: pl.semaphore_signal(
                esem.at[j], inc=1, device_id=(me_w - offs[j], me_x), device_id_type=MESH
            )
        )
    tcopies = [
        pltpu.make_async_remote_copy(
            src_ref=tokb.at[me_x], dst_ref=tokb.at[me_x], send_sem=tsend.at[d - 1], recv_sem=trecv.at[d - 1],
            device_id=(me_w, lax.rem(me_x + d, narrow)), device_id_type=MESH,
        )
        for d in range(1, narrow)
    ]
    local[0].wait()
    for copy in tcopies:
        copy.start()
    local[2].wait()
    wqb[...] = wqkb[:, 0, :]
    local[1].wait()
    for copy in tcopies:
        copy.wait_recv()

    floats = [tokb[i].astype(jnp.float32) for i in range(narrow)]
    square = functools.reduce(
        jnp.add, [jnp.sum(f * f, axis=-1, keepdims=True) for f in floats]
    )
    scale = lax.rsqrt(square / (narrow * width) + 1e-06)
    normed = [
        (floats[i] * scale * gainb[:, i * width:(i + 1) * width]).astype(jnp.bfloat16)
        for i in range(narrow)
    ]

    def project(weight):
        return functools.reduce(
            jnp.add,
            [
                jnp.dot(
                    normed[i], weight(i * width, (i + 1) * width),
                    preferred_element_type=jnp.float32,
                )
                for i in range(narrow)
            ],
        ).astype(jnp.bfloat16)

    query = project(lambda a, b: wqb[a:b])
    qin[0] = query

    def query_copy(source, o, j):
        return pltpu.make_async_remote_copy(
            src_ref=qin.at[source], dst_ref=qin.at[j], send_sem=qsend.at[j], recv_sem=qrecv.at[j],
            device_id=(lax.rem(me_w + o, wide), me_x), device_id_type=MESH,
        )

    qcopies = {j: query_copy(0, offs[j], j) for j in direct + relayed}
    relays = {j: query_copy(2, offs[j] - offs[2], j) for j in relayed}

    def known(j):
        pl.when(me_w + offs[j] >= wide if j > 1 else led == 1)(qcopies[j].start)

    def unknown(j):
        @pl.when(me_w + offs[j] < wide if j > 1 else led == 0)
        def _():
            pl.semaphore_wait(esem.at[j], 1)
            qcopies[j].start()

    for j in relayed + direct:
        known(j)
    for j in (1, 2, 3):
        unknown(j)

    lane = lax.broadcasted_iota(jnp.int32, (tcount, 128), 1)
    head_of = lax.broadcasted_iota(jnp.int32, (tcount, width), 1) // HEAD_DIM

    def stat_tile(columns, base, start):
        tile = start
        for h, column in enumerate(columns):
            tile = jnp.where(lane == base + h, column, tile)
        return tile

    local[4].wait()
    local[5].wait()
    local[6].wait()
    row = lax.broadcasted_iota(jnp.int32, (tcount, span), 0)
    place = lax.broadcasted_iota(jnp.int32, (tcount, span), 1) - row * page_len

    def offset(j):
        return (j - j % 2) * stride_len + j % 2

    def attend(j):
        home = lax.rem(me_w + (wide - offset(j)), wide) * tcount
        q = qin[j].astype(jnp.float32)
        spread = jnp.concatenate(
            [jnp.where(head_of == h, q, 0.0) for h in range(heads)], axis=0
        ).astype(jnp.bfloat16)
        slots = [ptb[j, home + r] for r in range(tcount)]
        keys = jnp.concatenate([kvb[s, 0] for s in slots], axis=0)
        values = jnp.concatenate([kvb[s, 1] for s in slots], axis=0)
        limit = jnp.full((tcount, span), 0, jnp.int32)
        for r in range(tcount):
            limit = jnp.where(
                row == r, jnp.minimum(lenb[home + r] - j * page_len, page_len), limit
            )
        valid1 = (place >= 0) & (place < limit)
        valid = jnp.concatenate([valid1] * heads, axis=0)
        scores = lax.dot_general(
            spread, keys, (((1,), (1,)), ((), ())), preferred_element_type=jnp.float32
        )
        scores = jnp.where(valid, scores, NEG)
        top = jnp.max(scores, axis=-1, keepdims=True)
        weights = jnp.where(valid, jnp.exp(scores - top), 0.0)
        total = jnp.sum(weights, axis=-1, keepdims=True)
        acc = jnp.dot(weights.astype(jnp.bfloat16), values, preferred_element_type=jnp.float32)
        mine = jnp.zeros((tcount, width), jnp.float32)
        for h in range(heads):
            mine = jnp.where(head_of == h, acc[h * tcount:(h + 1) * tcount], mine)
        stats = stat_tile(
            [top[h * tcount:(h + 1) * tcount] for h in range(heads)],
            0, jnp.full((tcount, 128), 0.0, jnp.float32),
        )
        stats = stat_tile(
            [total[h * tcount:(h + 1) * tcount] for h in range(heads)], 64, stats
        )
        return mine, stats

    def partial_copy(j):
        return pltpu.make_async_remote_copy(
            src_ref=pout.at[j], dst_ref=pin.at[j], send_sem=psend.at[j], recv_sem=precv.at[j],
            device_id=(lax.rem(me_w + (wide - offset(j)), wide), me_x), device_id_type=MESH,
        )

    def keep(ref, j, result):
        ref[j, :, :width] = result[0]
        ref[j, :, width:] = result[1]

    for j in direct[3:]:
        unknown(j)

    relay = (me_w + wide - offs[2]) // wide * ((2 * wide + offs[2] - offs[4] - 1 - me_w) // wide)

    @pl.when(relay > 0)
    def _():
        qcopies[2].wait_recv()
        relays[4].start()
        pl.when(me_w < wide + offs[2] - offs[5])(relays[5].start)

    def digits(order):
        return sum(j * 8**at for at, j in enumerate(order))

    part, quarter = me_w * 4 // wide, wide // 4
    row_first = 1 - (in_row + row_len - 1) // row_len
    part_first = 1 - (lax.rem(me_w, quarter) + quarter - 1) // quarter
    code = 0
    for at, orders in enumerate(ORDERS):
        inside, start, edge = (digits(order) for order in orders)
        here = 1 - (lax.rem(part - at + 4, 4) + 3) // 4
        code = code + here * (inside + row_first * (start - inside) + part_first * (edge - start))

    def page(step, code):
        j = lax.rem(code, 8)
        pl.when((j != 2) | (relay == 0))(query_copy(0, offs[2], j).wait_recv)
        keep(pout, j, attend(j))
        partial_copy(j).start()
        return code // 8

    lax.fori_loop(0, pages - 1, page, code)
    keep(pin, 0, attend(0))
    new_keys = project(lambda a, b: wqkb[a:b, 1, :]).astype(jnp.float32)
    local[3].wait()
    new_values = project(lambda a, b: wvb[a:b, :]).astype(jnp.float32)
    products = query.astype(jnp.float32) * new_keys
    self_score = stat_tile(
        [
            jnp.sum(jnp.where(head_of == h, products, 0.0), axis=-1, keepdims=True)
            for h in range(heads)
        ],
        0, jnp.full((tcount, 128), NEG, jnp.float32),
    )
    for j in range(1, pages):
        partial_copy(j).wait_recv()

    stats = [pin[j, :, width:] for j in range(pages)]
    best = functools.reduce(jnp.maximum, stats, self_score)
    self_factor = jnp.exp(self_score - best)
    factors = [jnp.exp(s - best) for s in stats]
    denom = self_factor
    for j in range(pages):
        denom = denom + factors[j] * pltpu.roll(stats[j], 64, 1)

    def widen(tile):
        wide_tile = jnp.zeros((tcount, width), jnp.float32)
        for h in range(heads):
            wide_tile = jnp.where(head_of == h, tile[:, h:h + 1], wide_tile)
        return wide_tile

    numer = widen(self_factor) * new_values
    for j in range(pages):
        numer = numer + widen(factors[j]) * pin[j, :, :width]
    heads_out = (numer / widen(denom)).astype(jnp.bfloat16)

    local[7].wait()
    rcopies = []
    for d in range(1, narrow):
        peer = lax.rem(me_x + d, narrow)
        start = pl.multiple_of(peer * width, width)
        rsout[d - 1] = jnp.dot(
            heads_out, wob[:, pl.ds(start, width)], preferred_element_type=jnp.float32
        )
        copy = pltpu.make_async_remote_copy(
            src_ref=rsout.at[d - 1], dst_ref=rsin.at[d - 1],
            send_sem=rsend.at[d - 1], recv_sem=rrecv.at[d - 1],
            device_id=(me_w, peer), device_id_type=MESH,
        )
        copy.start()
        rcopies.append(copy)
    start = pl.multiple_of(me_x * width, width)
    total = jnp.dot(heads_out, wob[:, pl.ds(start, width)], preferred_element_type=jnp.float32)
    for d in range(1, narrow):
        rcopies[d - 1].wait_recv()
        total = total + rsin[d - 1]
    outb[...] = total.astype(out.dtype)
    last = pltpu.make_async_copy(outb, out, lsem.at[0])
    last.start()
    last.wait()
    for copy in tcopies + rcopies + [partial_copy(j) for j in range(1, pages)]:
        copy.wait_send()
    for j in direct:
        qcopies[j].wait_send()
    for j in relayed:
        pl.when(me_w + offs[j] >= wide)(qcopies[j].wait_send)
        pl.when((relay > 0) & (me_w < wide + offs[2] - offs[j]))(relays[j].wait_send)


def body(wide, narrow, tokens, norm_gain, w_qk, w_value, w_out, kv_cache, cache_len, page_table):
    tcount, width = tokens.shape
    total, pages = page_table.shape
    features = norm_gain.shape[0]
    stride_len = wide // pages
    anywhere = pl.BlockSpec(memory_space=pltpu.HBM)
    dma = pltpu.SemaphoreType.DMA
    return pl.pallas_call(
        functools.partial(layer_kernel, wide, narrow, stride_len, wide // 16),
        out_shape=jax.ShapeDtypeStruct((tcount, width), jnp.bfloat16),
        in_specs=[anywhere] * 8,
        out_specs=pl.BlockSpec(memory_space=pl.ANY),
        scratch_shapes=[
            pltpu.VMEM((narrow, tcount, width), jnp.bfloat16),
            pltpu.VMEM((1, features), jnp.float32),
            pltpu.VMEM(w_qk.shape, jnp.bfloat16),
            pltpu.VMEM((features, width), jnp.bfloat16),
            pltpu.VMEM(w_value.shape, jnp.bfloat16),
            pltpu.VMEM(w_out.shape, jnp.bfloat16),
            pltpu.VMEM(kv_cache.shape, jnp.bfloat16),
            pltpu.SMEM((total,), jnp.int32),
            pltpu.SMEM((pages, total), jnp.int32),
            pltpu.VMEM((pages, tcount, width), jnp.bfloat16),
            pltpu.VMEM((pages, tcount, width + 128), jnp.float32),
            pltpu.VMEM((pages, tcount, width + 128), jnp.float32),
            pltpu.VMEM((narrow - 1, tcount, width), jnp.float32),
            pltpu.VMEM((narrow - 1, tcount, width), jnp.float32),
            dma((8,)),
            dma((narrow - 1,)), dma((narrow - 1,)),
            dma((pages,)), dma((pages,)),
            dma((pages,)), dma((pages,)),
            dma((narrow - 1,)), dma((narrow - 1,)),
            pltpu.SemaphoreType.REGULAR((pages,)),
            pltpu.VMEM((tcount, width), jnp.bfloat16),
        ],
        compiler_params=pltpu.CompilerParams(
            collective_id=0, has_side_effects=True, vmem_limit_bytes=62 << 20
        ),
    )(
        tokens, norm_gain.reshape(1, features), w_qk, w_value, w_out, kv_cache, cache_len,
        page_table.T,
    )


def solution(mesh):
    placed = (
        P("wide", "narrow"),
        P(),
        P(None, None, "narrow"),
        P(None, "narrow"),
        P("narrow", None),
        P("wide", None, None, "narrow"),
        P(),
        P(),
    )
    return jax.shard_map(
        functools.partial(body, mesh.shape["wide"], mesh.shape["narrow"]),
        mesh=mesh, in_specs=placed, out_specs=P("wide", "narrow"), check_vma=False,
    )
```

```python
import functools

import jax
import jax.numpy as jnp
from jax import lax
from jax.experimental import pallas as pl
from jax.experimental.pallas import tpu as pltpu
from jax.sharding import PartitionSpec as P

HEAD_DIM = 64
MESH = pl.DeviceIdType.MESH
ORDERS = (
    ((1, 6, 7, 2, 3, 4, 5), (1, 6, 7, 2, 3, 4, 5), (6, 7, 2, 3, 4, 5, 1)),
    ((1, 2, 3, 6, 7, 4, 5), (1, 2, 3, 6, 7, 4, 5), (1, 2, 7, 6, 3, 4, 5)),
    ((4, 5, 2, 3, 1, 6, 7), (4, 2, 5, 3, 1, 6, 7), (4, 2, 3, 1, 7, 6, 5)),
    ((6, 7, 1, 4, 5, 2, 3), (6, 1, 4, 7, 5, 2, 3), (6, 4, 3, 5, 2, 1, 7)),
)
NEG = -1e30


def layer_kernel(
    wide, narrow, stride_len, row_len,
    tok, gain, wqk, wv, wo, kv, clen, ptab, out,
    tokb, gainb, wqkb, wqb, wvb, wob, kvb, lenb, ptb, qin, pout, pin, rsout,
    lsem, tsend, trecv, qsend, qrecv, psend, precv, rsend, rrecv, esem,
):
    me_w = lax.axis_index("wide")
    me_x = lax.axis_index("narrow")
    tcount, width = tok.shape
    pages = ptab.shape[0]
    offs = tuple((j - j % 2) * stride_len + j % 2 for j in range(pages))
    direct, relayed, answer_order = (1, 2, 3, 6, 7), (4, 5), (2, 3, 6, 7, 1)
    heads = width // HEAD_DIM
    page_len = kvb.shape[2]
    span = tcount * page_len

    local = [
        pltpu.make_async_copy(tok, tokb.at[me_x], lsem.at[0]),
        pltpu.make_async_copy(gain, gainb, lsem.at[1]),
        pltpu.make_async_copy(wqk, wqkb, lsem.at[2]),
        pltpu.make_async_copy(wv, wvb, lsem.at[3]),
        pltpu.make_async_copy(clen, lenb, lsem.at[4]),
        pltpu.make_async_copy(ptab, ptb, lsem.at[5]),
        pltpu.make_async_copy(kv, kvb, lsem.at[6]),
        pltpu.make_async_copy(wo, wob, lsem.at[7]),
    ]

    barrier = pltpu.get_barrier_semaphore()

    def greet(target):
        pl.semaphore_signal(barrier, inc=1, device_id=target, device_id_type=MESH)

    expected = narrow - 1
    for d in range(1, narrow):
        greet((me_w, lax.rem(me_x + d, narrow)))
    for j in direct[1:]:
        pl.when(me_w + offs[j] < wide)(lambda j=j: greet((me_w + offs[j], me_x)))
        pl.when(me_w < offs[j])(lambda j=j: greet((me_w + wide - offs[j], me_x)))
        expected = expected + (me_w + wide - offs[j]) // wide + (me_w + offs[j]) // wide
    for j in relayed:
        pl.when(me_w < offs[j])(lambda j=j: greet((me_w + wide - offs[j], me_x)))
        expected = expected + (me_w + offs[j]) // wide
    ahead, behind = lax.rem(me_w + 1, wide), lax.rem(me_w + wide - 1, wide)
    in_row = lax.rem(me_w, row_len)
    led = in_row // (row_len - 1) * (me_w // (wide // 2))
    leads = (1 - (in_row + row_len - 1) // row_len) * (behind // (wide // 2))
    pl.when(led == 0)(lambda: greet((ahead, me_x)))
    pl.when(leads == 1)(lambda: greet((behind, me_x)))
    expected = expected + 1 - leads + led
    for copy in local:
        copy.start()
    pl.semaphore_wait(barrier, expected)
    for j in answer_order:
        pl.when(me_w >= offs[j] if j > 1 else leads == 0)(
            lambda j=j: pl.semaphore_signal(
                esem.at[j], inc=1, device_id=(me_w - offs[j], me_x), device_id_type=MESH
            )
        )
    tcopies = [
        pltpu.make_async_remote_copy(
            src_ref=tokb.at[me_x], dst_ref=tokb.at[me_x], send_sem=tsend.at[d - 1], recv_sem=trecv.at[d - 1],
            device_id=(me_w, lax.rem(me_x + d, narrow)), device_id_type=MESH,
        )
        for d in range(1, narrow)
    ]
    far_first = sorted(range(1, narrow), key=lambda d: -min(d, narrow - d))
    local[0].wait()
    for d in far_first:
        tcopies[d - 1].start()
    local[2].wait()
    wqb[...] = wqkb[:, 0, :]
    local[1].wait()
    for copy in tcopies:
        copy.wait_recv()

    floats = [tokb[i].astype(jnp.float32) for i in range(narrow)]
    square = functools.reduce(
        jnp.add, [jnp.sum(f * f, axis=-1, keepdims=True) for f in floats]
    )
    scale = lax.rsqrt(square / (narrow * width) + 1e-06)
    normed = [
        (floats[i] * scale * gainb[:, i * width:(i + 1) * width]).astype(jnp.bfloat16)
        for i in range(narrow)
    ]

    def project(weight):
        return functools.reduce(
            jnp.add,
            [
                jnp.dot(
                    normed[i], weight(i * width, (i + 1) * width),
                    preferred_element_type=jnp.float32,
                )
                for i in range(narrow)
            ],
        ).astype(jnp.bfloat16)

    query = project(lambda a, b: wqb[a:b])
    qin[0] = query

    def query_copy(source, o, j):
        return pltpu.make_async_remote_copy(
            src_ref=qin.at[source], dst_ref=qin.at[j], send_sem=qsend.at[j], recv_sem=qrecv.at[j],
            device_id=(lax.rem(me_w + o, wide), me_x), device_id_type=MESH,
        )

    qcopies = {j: query_copy(0, offs[j], j) for j in direct + relayed}
    quarter = wide // 4
    relay = (wide - 1 - me_w) // (2 * quarter)
    back = relay * (1 - me_w // quarter)
    source = 2 + 4 * back
    relays = {
        4: query_copy(source, offs[2] + back * (offs[6] - offs[2]), 4),
        5: query_copy(source, offs[3] + back * (offs[7] - offs[3]), 5),
    }
    relay_odd = (relay > 0) & (me_w != quarter - 1)

    def known(j):
        pl.when(me_w + offs[j] >= wide if j > 1 else led == 1)(qcopies[j].start)

    def unknown(j):
        @pl.when(me_w + offs[j] < wide if j > 1 else led == 0)
        def _():
            pl.semaphore_wait(esem.at[j], 1)
            qcopies[j].start()

    for j in relayed + direct:
        known(j)
    for j in (1, 2, 3):
        unknown(j)

    lane = lax.broadcasted_iota(jnp.int32, (tcount, 128), 1)
    head_of = lax.broadcasted_iota(jnp.int32, (tcount, width), 1) // HEAD_DIM

    def stat_tile(columns, base, start):
        tile = start
        for h, column in enumerate(columns):
            tile = jnp.where(lane == base + h, column, tile)
        return tile

    local[4].wait()
    local[5].wait()
    local[6].wait()
    row = lax.broadcasted_iota(jnp.int32, (tcount, span), 0)
    place = lax.broadcasted_iota(jnp.int32, (tcount, span), 1) - row * page_len

    def offset(j):
        return (j - j % 2) * stride_len + j % 2

    def attend(j):
        home = lax.rem(me_w + (wide - offset(j)), wide) * tcount
        q = qin[j].astype(jnp.float32)
        spread = jnp.concatenate(
            [jnp.where(head_of == h, q, 0.0) for h in range(heads)], axis=0
        ).astype(jnp.bfloat16)
        slots = [ptb[j, home + r] for r in range(tcount)]
        keys = jnp.concatenate([kvb[s, 0] for s in slots], axis=0)
        values = jnp.concatenate([kvb[s, 1] for s in slots], axis=0)
        limit = jnp.full((tcount, span), 0, jnp.int32)
        for r in range(tcount):
            limit = jnp.where(
                row == r, jnp.minimum(lenb[home + r] - j * page_len, page_len), limit
            )
        valid1 = (place >= 0) & (place < limit)
        valid = jnp.concatenate([valid1] * heads, axis=0)
        scores = lax.dot_general(
            spread, keys, (((1,), (1,)), ((), ())), preferred_element_type=jnp.float32
        )
        scores = jnp.where(valid, scores, NEG)
        top = jnp.max(scores, axis=-1, keepdims=True)
        weights = jnp.where(valid, jnp.exp(scores - top), 0.0)
        total = jnp.sum(weights, axis=-1, keepdims=True)
        acc = jnp.dot(weights.astype(jnp.bfloat16), values, preferred_element_type=jnp.float32)
        mine = jnp.zeros((tcount, width), jnp.float32)
        for h in range(heads):
            mine = jnp.where(head_of == h, acc[h * tcount:(h + 1) * tcount], mine)
        stats = stat_tile(
            [top[h * tcount:(h + 1) * tcount] for h in range(heads)],
            0, jnp.full((tcount, 128), 0.0, jnp.float32),
        )
        stats = stat_tile(
            [total[h * tcount:(h + 1) * tcount] for h in range(heads)], 64, stats
        )
        return mine, stats

    def partial_copy(j):
        return pltpu.make_async_remote_copy(
            src_ref=pout.at[j], dst_ref=pin.at[j], send_sem=psend.at[j], recv_sem=precv.at[j],
            device_id=(lax.rem(me_w + (wide - offset(j)), wide), me_x), device_id_type=MESH,
        )

    def keep(ref, j, result):
        ref[j, :, :width] = result[0]
        ref[j, :, width:] = result[1]

    for j in direct[3:]:
        unknown(j)

    @pl.when(relay > 0)
    def _():
        query_copy(0, offs[2], source).wait_recv()
        relays[4].start()
        pl.when(relay_odd)(relays[5].start)

    def digits(order):
        return sum(j * 8**at for at, j in enumerate(order))

    part = me_w // quarter
    row_first = 1 - (in_row + row_len - 1) // row_len
    part_first = 1 - (lax.rem(me_w, quarter) + quarter - 1) // quarter
    code = 0
    for at, orders in enumerate(ORDERS):
        inside, start, edge = (digits(order) for order in orders)
        here = 1 - (lax.rem(part - at + 4, 4) + 3) // 4
        code = code + here * (inside + row_first * (start - inside) + part_first * (edge - start))

    def page(step, code):
        j = lax.rem(code, 8)
        pl.when((j != source) | (relay == 0))(query_copy(0, offs[2], j).wait_recv)
        keep(pout, j, attend(j))
        partial_copy(j).start()
        return code // 8

    lax.fori_loop(0, pages - 1, page, code)
    keep(pin, 0, attend(0))
    new_keys = project(lambda a, b: wqkb[a:b, 1, :]).astype(jnp.float32)
    local[3].wait()
    new_values = project(lambda a, b: wvb[a:b, :]).astype(jnp.float32)
    products = query.astype(jnp.float32) * new_keys
    self_score = stat_tile(
        [
            jnp.sum(jnp.where(head_of == h, products, 0.0), axis=-1, keepdims=True)
            for h in range(heads)
        ],
        0, jnp.full((tcount, 128), NEG, jnp.float32),
    )
    for j in range(1, pages):
        partial_copy(j).wait_recv()

    stats = [pin[j, :, width:] for j in range(pages)]
    best = functools.reduce(jnp.maximum, stats, self_score)
    self_factor = jnp.exp(self_score - best)
    factors = [jnp.exp(s - best) for s in stats]
    denom = self_factor
    for j in range(pages):
        denom = denom + factors[j] * pltpu.roll(stats[j], 64, 1)

    def widen(tile):
        wide_tile = jnp.zeros((tcount, width), jnp.float32)
        for h in range(heads):
            wide_tile = jnp.where(head_of == h, tile[:, h:h + 1], wide_tile)
        return wide_tile

    numer = widen(self_factor) * new_values
    for j in range(pages):
        numer = numer + widen(factors[j]) * pin[j, :, :width]
    heads_out = (numer / widen(denom)).astype(jnp.bfloat16)

    local[7].wait()
    rcopies = []
    for d in far_first:
        peer = lax.rem(me_x + d, narrow)
        start = pl.multiple_of(peer * width, width)
        rsout[d - 1] = jnp.dot(
            heads_out, wob[:, pl.ds(start, width)], preferred_element_type=jnp.float32
        )
        copy = pltpu.make_async_remote_copy(
            src_ref=rsout.at[d - 1], dst_ref=out.at[d - 1],
            send_sem=rsend.at[d - 1], recv_sem=rrecv.at[d - 1],
            device_id=(me_w, peer), device_id_type=MESH,
        )
        copy.start()
        rcopies.append(copy)
    start = pl.multiple_of(me_x * width, width)
    rsout[narrow - 1] = jnp.dot(
        heads_out, wob[:, pl.ds(start, width)], preferred_element_type=jnp.float32
    )
    own = pltpu.make_async_copy(rsout.at[narrow - 1], out.at[narrow - 1], lsem.at[0])
    own.start()
    for copy in tcopies + [partial_copy(j) for j in range(1, pages)]:
        copy.wait_send()
    for j in direct:
        qcopies[j].wait_send()
    for j in relayed:
        pl.when(me_w + offs[j] >= wide)(qcopies[j].wait_send)
    pl.when(relay > 0)(relays[4].wait_send)
    pl.when(relay_odd)(relays[5].wait_send)
    own.wait()
    for copy in rcopies:
        copy.wait()


def body(wide, narrow, tokens, norm_gain, w_qk, w_value, w_out, kv_cache, cache_len, page_table):
    tcount, width = tokens.shape
    total, pages = page_table.shape
    features = norm_gain.shape[0]
    stride_len = wide // pages
    anywhere = pl.BlockSpec(memory_space=pltpu.HBM)
    dma = pltpu.SemaphoreType.DMA
    sums = pl.pallas_call(
        functools.partial(layer_kernel, wide, narrow, stride_len, wide // 16),
        out_shape=jax.ShapeDtypeStruct((narrow, tcount, width), jnp.float32),
        in_specs=[anywhere] * 8,
        out_specs=pl.BlockSpec(memory_space=pl.ANY),
        scratch_shapes=[
            pltpu.VMEM((narrow, tcount, width), jnp.bfloat16),
            pltpu.VMEM((1, features), jnp.float32),
            pltpu.VMEM(w_qk.shape, jnp.bfloat16),
            pltpu.VMEM((features, width), jnp.bfloat16),
            pltpu.VMEM(w_value.shape, jnp.bfloat16),
            pltpu.VMEM(w_out.shape, jnp.bfloat16),
            pltpu.VMEM(kv_cache.shape, jnp.bfloat16),
            pltpu.SMEM((total,), jnp.int32),
            pltpu.SMEM((pages, total), jnp.int32),
            pltpu.VMEM((pages, tcount, width), jnp.bfloat16),
            pltpu.VMEM((pages, tcount, width + 128), jnp.float32),
            pltpu.VMEM((pages, tcount, width + 128), jnp.float32),
            pltpu.VMEM((narrow, tcount, width), jnp.float32),
            dma((8,)),
            dma((narrow - 1,)), dma((narrow - 1,)),
            dma((pages,)), dma((pages,)),
            dma((pages,)), dma((pages,)),
            dma((narrow - 1,)), dma((narrow - 1,)),
            pltpu.SemaphoreType.REGULAR((pages,)),
        ],
        compiler_params=pltpu.CompilerParams(
            collective_id=0, has_side_effects=True, vmem_limit_bytes=62 << 20
        ),
    )(
        tokens, norm_gain.reshape(1, features), w_qk, w_value, w_out, kv_cache, cache_len,
        page_table.T,
    )
    return jnp.sum(sums, axis=0).astype(jnp.bfloat16)


def solution(mesh):
    placed = (
        P("wide", "narrow"),
        P(),
        P(None, None, "narrow"),
        P(None, "narrow"),
        P("narrow", None),
        P("wide", None, None, "narrow"),
        P(),
        P(),
    )
    return jax.shard_map(
        functools.partial(body, mesh.shape["wide"], mesh.shape["narrow"]),
        mesh=mesh, in_specs=placed, out_specs=P("wide", "narrow"), check_vma=False,
    )
```

```python
import functools

import jax
import jax.numpy as jnp
from jax import lax
from jax.experimental import pallas as pl
from jax.experimental.pallas import tpu as pltpu
from jax.sharding import PartitionSpec as P

HEAD_DIM = 64
MESH = pl.DeviceIdType.MESH
ORDERS = (
    ((1, 6, 7, 2, 3, 4, 5), (1, 6, 7, 2, 3, 4, 5), (6, 7, 2, 3, 4, 5, 1)),
    ((1, 2, 3, 6, 7, 4, 5), (1, 2, 3, 6, 7, 4, 5), (1, 2, 7, 6, 3, 4, 5)),
    ((4, 5, 2, 3, 1, 6, 7), (4, 2, 5, 3, 1, 6, 7), (4, 2, 3, 1, 7, 6, 5)),
    ((6, 7, 1, 4, 5, 2, 3), (6, 1, 4, 7, 5, 2, 3), (6, 4, 3, 5, 2, 1, 7)),
)
NEG = -1e30


def layer_kernel(
    wide, narrow, stride_len, row_len,
    tok, gain, wqk, wv, wo, kv, clen, ptab, out,
    tokb, gainb, wqkb, wqb, wvb, wob, kvb, lenb, ptb, qin, pout, pin, rsout,
    lsem, tsend, trecv, qsend, qrecv, psend, precv, rsend, rrecv, esem, newb, selfb,
):
    me_w = lax.axis_index("wide")
    me_x = lax.axis_index("narrow")
    tcount, width = tok.shape
    pages = ptab.shape[0]
    offs = tuple((j - j % 2) * stride_len + j % 2 for j in range(pages))
    direct, relayed, answer_order = (1, 2, 3, 6, 7), (4, 5), (2, 3, 6, 7, 1)
    heads = width // HEAD_DIM
    page_len = kvb.shape[2]
    span = tcount * page_len

    local = [
        pltpu.make_async_copy(tok, tokb.at[me_x], lsem.at[0]),
        pltpu.make_async_copy(gain, gainb, lsem.at[1]),
        pltpu.make_async_copy(wqk, wqkb, lsem.at[2]),
        pltpu.make_async_copy(wv, wvb, lsem.at[3]),
        pltpu.make_async_copy(clen, lenb, lsem.at[4]),
        pltpu.make_async_copy(ptab, ptb, lsem.at[5]),
        pltpu.make_async_copy(kv, kvb, lsem.at[6]),
        pltpu.make_async_copy(wo, wob, lsem.at[7]),
    ]

    barrier = pltpu.get_barrier_semaphore()

    def greet(target):
        pl.semaphore_signal(barrier, inc=1, device_id=target, device_id_type=MESH)

    expected = narrow - 1
    for d in range(1, narrow):
        greet((me_w, lax.rem(me_x + d, narrow)))
    for j in direct[1:]:
        pl.when(me_w + offs[j] < wide)(lambda j=j: greet((me_w + offs[j], me_x)))
        pl.when(me_w < offs[j])(lambda j=j: greet((me_w + wide - offs[j], me_x)))
        expected = expected + (me_w + wide - offs[j]) // wide + (me_w + offs[j]) // wide
    for j in relayed:
        pl.when(me_w < offs[j])(lambda j=j: greet((me_w + wide - offs[j], me_x)))
        expected = expected + (me_w + offs[j]) // wide
    ahead, behind = lax.rem(me_w + 1, wide), lax.rem(me_w + wide - 1, wide)
    in_row = lax.rem(me_w, row_len)
    led = in_row // (row_len - 1) * (me_w // (wide // 2))
    leads = (1 - (in_row + row_len - 1) // row_len) * (behind // (wide // 2))
    pl.when(led == 0)(lambda: greet((ahead, me_x)))
    pl.when(leads == 1)(lambda: greet((behind, me_x)))
    expected = expected + 1 - leads + led
    for copy in local:
        copy.start()
    pl.semaphore_wait(barrier, expected)
    for j in answer_order:
        pl.when(me_w >= offs[j] if j > 1 else leads == 0)(
            lambda j=j: pl.semaphore_signal(
                esem.at[j], inc=1, device_id=(me_w - offs[j], me_x), device_id_type=MESH
            )
        )
    tcopies = [
        pltpu.make_async_remote_copy(
            src_ref=tokb.at[me_x], dst_ref=tokb.at[me_x], send_sem=tsend.at[d - 1], recv_sem=trecv.at[d - 1],
            device_id=(me_w, lax.rem(me_x + d, narrow)), device_id_type=MESH,
        )
        for d in range(1, narrow)
    ]
    far_first = sorted(range(1, narrow), key=lambda d: -min(d, narrow - d))
    local[0].wait()
    for d in far_first:
        tcopies[d - 1].start()
    local[2].wait()
    wqb[...] = wqkb[:, 0, :]
    local[1].wait()
    for copy in tcopies:
        copy.wait_recv()

    floats = [tokb[i].astype(jnp.float32) for i in range(narrow)]
    square = functools.reduce(
        jnp.add, [jnp.sum(f * f, axis=-1, keepdims=True) for f in floats]
    )
    scale = lax.rsqrt(square / (narrow * width) + 1e-06)
    normed = [
        (floats[i] * scale * gainb[:, i * width:(i + 1) * width]).astype(jnp.bfloat16)
        for i in range(narrow)
    ]

    def project(weight):
        return functools.reduce(
            jnp.add,
            [
                jnp.dot(
                    normed[i], weight(i * width, (i + 1) * width),
                    preferred_element_type=jnp.float32,
                )
                for i in range(narrow)
            ],
        ).astype(jnp.bfloat16)

    query = project(lambda a, b: wqb[a:b])
    qin[0] = query

    def query_copy(source, o, j):
        return pltpu.make_async_remote_copy(
            src_ref=qin.at[source], dst_ref=qin.at[j], send_sem=qsend.at[j], recv_sem=qrecv.at[j],
            device_id=(lax.rem(me_w + o, wide), me_x), device_id_type=MESH,
        )

    qcopies = {j: query_copy(0, offs[j], j) for j in direct + relayed}
    quarter = wide // 4
    relay = (wide - 1 - me_w) // (2 * quarter)
    back = relay * (1 - me_w // quarter)
    source = 2 + 4 * back
    relays = {
        4: query_copy(source, offs[2] + back * (offs[6] - offs[2]), 4),
        5: query_copy(source, offs[3] + back * (offs[7] - offs[3]), 5),
    }
    relay_odd = (relay > 0) & (me_w != quarter - 1)

    def known(j):
        pl.when(me_w + offs[j] >= wide if j > 1 else led == 1)(qcopies[j].start)

    def unknown(j):
        @pl.when(me_w + offs[j] < wide if j > 1 else led == 0)
        def _():
            pl.semaphore_wait(esem.at[j], 1)
            qcopies[j].start()

    for j in relayed + direct:
        known(j)
    for j in (1, 2, 3):
        unknown(j)

    lane = lax.broadcasted_iota(jnp.int32, (tcount, 128), 1)
    head_of = lax.broadcasted_iota(jnp.int32, (tcount, width), 1) // HEAD_DIM

    def stat_tile(columns, base, start):
        tile = start
        for h, column in enumerate(columns):
            tile = jnp.where(lane == base + h, column, tile)
        return tile

    local[4].wait()
    local[5].wait()
    local[6].wait()
    row = lax.broadcasted_iota(jnp.int32, (tcount, span), 0)
    place = lax.broadcasted_iota(jnp.int32, (tcount, span), 1) - row * page_len

    def offset(j):
        return (j - j % 2) * stride_len + j % 2

    def attend(j):
        home = lax.rem(me_w + (wide - offset(j)), wide) * tcount
        q = qin[j].astype(jnp.float32)
        spread = jnp.concatenate(
            [jnp.where(head_of == h, q, 0.0) for h in range(heads)], axis=0
        ).astype(jnp.bfloat16)
        slots = [ptb[j, home + r] for r in range(tcount)]
        keys = jnp.concatenate([kvb[s, 0] for s in slots], axis=0)
        values = jnp.concatenate([kvb[s, 1] for s in slots], axis=0)
        limit = jnp.full((tcount, span), 0, jnp.int32)
        for r in range(tcount):
            limit = jnp.where(
                row == r, jnp.minimum(lenb[home + r] - j * page_len, page_len), limit
            )
        valid1 = (place >= 0) & (place < limit)
        valid = jnp.concatenate([valid1] * heads, axis=0)
        scores = lax.dot_general(
            spread, keys, (((1,), (1,)), ((), ())), preferred_element_type=jnp.float32
        )
        scores = jnp.where(valid, scores, NEG)
        top = jnp.max(scores, axis=-1, keepdims=True)
        weights = jnp.where(valid, jnp.exp(scores - top), 0.0)
        total = jnp.sum(weights, axis=-1, keepdims=True)
        acc = jnp.dot(weights.astype(jnp.bfloat16), values, preferred_element_type=jnp.float32)
        mine = jnp.zeros((tcount, width), jnp.float32)
        for h in range(heads):
            mine = jnp.where(head_of == h, acc[h * tcount:(h + 1) * tcount], mine)
        stats = stat_tile(
            [top[h * tcount:(h + 1) * tcount] for h in range(heads)],
            0, jnp.full((tcount, 128), 0.0, jnp.float32),
        )
        stats = stat_tile(
            [total[h * tcount:(h + 1) * tcount] for h in range(heads)], 64, stats
        )
        return mine, stats

    def partial_copy(j):
        return pltpu.make_async_remote_copy(
            src_ref=pout.at[j], dst_ref=pin.at[j], send_sem=psend.at[j], recv_sem=precv.at[j],
            device_id=(lax.rem(me_w + (wide - offset(j)), wide), me_x), device_id_type=MESH,
        )

    def keep(ref, j, result):
        high = result[1].astype(jnp.bfloat16).astype(jnp.float32)
        middle = (result[1] - high).astype(jnp.bfloat16).astype(jnp.float32)
        terms = high + pltpu.roll(middle, 16, 1) + pltpu.roll(result[1] - high - middle, 32, 1)
        ref[j, :, :width] = result[0].astype(jnp.bfloat16)
        ref[j, :, width:] = terms.astype(jnp.bfloat16)

    def statistics(j):
        terms = pin[j, :, width:].astype(jnp.float32)
        return terms + (pltpu.roll(terms, 128 - 16, 1) + pltpu.roll(terms, 128 - 32, 1))

    def own_part():
        keep(pin, 0, attend(0))
        new_keys = project(lambda a, b: wqkb[a:b, 1, :]).astype(jnp.float32)
        local[3].wait()
        newb[...] = project(lambda a, b: wvb[a:b, :]).astype(jnp.float32)
        products = query.astype(jnp.float32) * new_keys
        selfb[...] = stat_tile(
            [
                jnp.sum(jnp.where(head_of == h, products, 0.0), axis=-1, keepdims=True)
                for h in range(heads)
            ],
            0, jnp.full((tcount, 128), NEG, jnp.float32),
        )

    part = me_w // quarter
    pl.when(part == 0)(own_part)
    for j in direct[3:]:
        unknown(j)

    @pl.when(relay > 0)
    def _():
        query_copy(0, offs[2], source).wait_recv()
        relays[4].start()
        pl.when(relay_odd)(relays[5].start)

    def digits(order):
        return sum(j * 8**at for at, j in enumerate(order))

    row_first = 1 - (in_row + row_len - 1) // row_len
    part_first = 1 - (lax.rem(me_w, quarter) + quarter - 1) // quarter
    code = 0
    for at, orders in enumerate(ORDERS):
        inside, start, edge = (digits(order) for order in orders)
        here = 1 - (lax.rem(part - at + 4, 4) + 3) // 4
        code = code + here * (inside + row_first * (start - inside) + part_first * (edge - start))

    def page(step, code):
        j = lax.rem(code, 8)
        pl.when((j != source) | (relay == 0))(query_copy(0, offs[2], j).wait_recv)
        keep(pout, j, attend(j))
        partial_copy(j).start()
        return code // 8

    lax.fori_loop(0, pages - 1, page, code)
    pl.when(part > 0)(own_part)
    for j in range(1, pages):
        partial_copy(j).wait_recv()

    self_score = selfb[...]
    stats = [statistics(j) for j in range(pages)]
    best = functools.reduce(jnp.maximum, stats, self_score)
    self_factor = jnp.exp(self_score - best)
    factors = [jnp.exp(s - best) for s in stats]
    denom = self_factor
    for j in range(pages):
        denom = denom + factors[j] * pltpu.roll(stats[j], 64, 1)

    def widen(tile):
        wide_tile = jnp.zeros((tcount, width), jnp.float32)
        for h in range(heads):
            wide_tile = jnp.where(head_of == h, tile[:, h:h + 1], wide_tile)
        return wide_tile

    numer = widen(self_factor) * newb[...]
    for j in range(pages):
        numer = numer + widen(factors[j]) * pin[j, :, :width].astype(jnp.float32)
    heads_out = (numer / widen(denom)).astype(jnp.bfloat16)

    local[7].wait()
    rcopies = []
    for d in far_first:
        peer = lax.rem(me_x + d, narrow)
        start = pl.multiple_of(peer * width, width)
        rsout[d - 1] = jnp.dot(
            heads_out, wob[:, pl.ds(start, width)], preferred_element_type=jnp.float32
        )
        copy = pltpu.make_async_remote_copy(
            src_ref=rsout.at[d - 1], dst_ref=out.at[d - 1],
            send_sem=rsend.at[d - 1], recv_sem=rrecv.at[d - 1],
            device_id=(me_w, peer), device_id_type=MESH,
        )
        copy.start()
        rcopies.append(copy)
    start = pl.multiple_of(me_x * width, width)
    rsout[narrow - 1] = jnp.dot(
        heads_out, wob[:, pl.ds(start, width)], preferred_element_type=jnp.float32
    )
    own = pltpu.make_async_copy(rsout.at[narrow - 1], out.at[narrow - 1], lsem.at[0])
    own.start()
    for copy in tcopies + [partial_copy(j) for j in range(1, pages)]:
        copy.wait_send()
    for j in direct:
        qcopies[j].wait_send()
    for j in relayed:
        pl.when(me_w + offs[j] >= wide)(qcopies[j].wait_send)
    pl.when(relay > 0)(relays[4].wait_send)
    pl.when(relay_odd)(relays[5].wait_send)
    own.wait()
    for copy in rcopies:
        copy.wait()


def body(wide, narrow, tokens, norm_gain, w_qk, w_value, w_out, kv_cache, cache_len, page_table):
    tcount, width = tokens.shape
    total, pages = page_table.shape
    features = norm_gain.shape[0]
    stride_len = wide // pages
    anywhere = pl.BlockSpec(memory_space=pltpu.HBM)
    dma = pltpu.SemaphoreType.DMA
    sums = pl.pallas_call(
        functools.partial(layer_kernel, wide, narrow, stride_len, wide // 16),
        out_shape=jax.ShapeDtypeStruct((narrow, tcount, width), jnp.float32),
        in_specs=[anywhere] * 8,
        out_specs=pl.BlockSpec(memory_space=pl.ANY),
        scratch_shapes=[
            pltpu.VMEM((narrow, tcount, width), jnp.bfloat16),
            pltpu.VMEM((1, features), jnp.float32),
            pltpu.VMEM(w_qk.shape, jnp.bfloat16),
            pltpu.VMEM((features, width), jnp.bfloat16),
            pltpu.VMEM(w_value.shape, jnp.bfloat16),
            pltpu.VMEM(w_out.shape, jnp.bfloat16),
            pltpu.VMEM(kv_cache.shape, jnp.bfloat16),
            pltpu.SMEM((total,), jnp.int32),
            pltpu.SMEM((pages, total), jnp.int32),
            pltpu.VMEM((pages, tcount, width), jnp.bfloat16),
            pltpu.VMEM((pages, tcount, width + 128), jnp.bfloat16),
            pltpu.VMEM((pages, tcount, width + 128), jnp.bfloat16),
            pltpu.VMEM((narrow, tcount, width), jnp.float32),
            dma((8,)),
            dma((narrow - 1,)), dma((narrow - 1,)),
            dma((pages,)), dma((pages,)),
            dma((pages,)), dma((pages,)),
            dma((narrow - 1,)), dma((narrow - 1,)),
            pltpu.SemaphoreType.REGULAR((pages,)),
            pltpu.VMEM((tcount, width), jnp.float32),
            pltpu.VMEM((tcount, 128), jnp.float32),
        ],
        compiler_params=pltpu.CompilerParams(
            collective_id=0, has_side_effects=True, vmem_limit_bytes=62 << 20
        ),
    )(
        tokens, norm_gain.reshape(1, features), w_qk, w_value, w_out, kv_cache, cache_len,
        page_table.T,
    )
    return jnp.sum(sums, axis=0).astype(jnp.bfloat16)


def solution(mesh):
    placed = (
        P("wide", "narrow"),
        P(),
        P(None, None, "narrow"),
        P(None, "narrow"),
        P("narrow", None),
        P("wide", None, None, "narrow"),
        P(),
        P(),
    )
    return jax.shard_map(
        functools.partial(body, mesh.shape["wide"], mesh.shape["narrow"]),
        mesh=mesh, in_specs=placed, out_specs=P("wide", "narrow"), check_vma=False,
    )
```

```python
import functools

import jax
import jax.numpy as jnp
from jax import lax
from jax.experimental import pallas as pl
from jax.experimental.pallas import tpu as pltpu
from jax.sharding import PartitionSpec as P

HEAD_DIM = 64
MESH = pl.DeviceIdType.MESH
ORDERS = (
    ((1, 6, 7, 2, 3, 4, 5), (1, 6, 7, 2, 3, 4, 5), (6, 7, 2, 3, 4, 5, 1)),
    ((1, 2, 3, 6, 7, 4, 5), (1, 2, 3, 6, 7, 4, 5), (1, 2, 7, 6, 3, 4, 5)),
    ((4, 5, 2, 3, 1, 6, 7), (4, 2, 5, 3, 1, 6, 7), (4, 2, 3, 1, 7, 6, 5)),
    ((6, 7, 1, 4, 5, 2, 3), (6, 1, 4, 7, 5, 2, 3), (6, 4, 3, 5, 2, 1, 7)),
)
NEG = -1e30


def layer_kernel(
    wide, narrow, stride_len, row_len,
    tok, gain, wqk, wv, wo, kv, clen, ptab, out,
    tokb, gainb, wqkb, wqb, wvb, wob, kvb, lenb, ptb, qin, pout, pin, rsout,
    lsem, tsend, trecv, qsend, qrecv, psend, precv, rsend, rrecv, esem, newb, selfb,
):
    me_w = lax.axis_index("wide")
    me_x = lax.axis_index("narrow")
    tcount, width = tok.shape
    pages = ptab.shape[0]
    offs = tuple((j - j % 2) * stride_len + j % 2 for j in range(pages))
    direct, relayed, answer_order = (1, 2, 3, 6, 7), (4, 5), (2, 3, 6, 7, 1)
    heads = width // HEAD_DIM
    page_len = kvb.shape[2]
    span = tcount * page_len

    local = [
        pltpu.make_async_copy(tok, tokb.at[me_x], lsem.at[0]),
        pltpu.make_async_copy(gain, gainb, lsem.at[1]),
        pltpu.make_async_copy(wqk, wqkb, lsem.at[2]),
        pltpu.make_async_copy(wv, wvb, lsem.at[3]),
        pltpu.make_async_copy(clen, lenb, lsem.at[4]),
        pltpu.make_async_copy(ptab, ptb, lsem.at[5]),
        pltpu.make_async_copy(kv, kvb, lsem.at[6]),
        pltpu.make_async_copy(wo, wob, lsem.at[7]),
    ]

    barrier = pltpu.get_barrier_semaphore()

    def greet(target):
        pl.semaphore_signal(barrier, inc=1, device_id=target, device_id_type=MESH)

    expected = narrow - 1
    for d in range(1, narrow):
        greet((me_w, lax.rem(me_x + d, narrow)))
    for j in direct[1:]:
        pl.when(me_w + offs[j] < wide)(lambda j=j: greet((me_w + offs[j], me_x)))
        pl.when(me_w < offs[j])(lambda j=j: greet((me_w + wide - offs[j], me_x)))
        expected = expected + (me_w + wide - offs[j]) // wide + (me_w + offs[j]) // wide
    for j in relayed:
        pl.when(me_w < offs[j])(lambda j=j: greet((me_w + wide - offs[j], me_x)))
        expected = expected + (me_w + offs[j]) // wide
    ahead, behind = lax.rem(me_w + 1, wide), lax.rem(me_w + wide - 1, wide)
    in_row = lax.rem(me_w, row_len)
    led = in_row // (row_len - 1) * (me_w // (wide // 2))
    leads = (1 - (in_row + row_len - 1) // row_len) * (behind // (wide // 2))
    pl.when(led == 0)(lambda: greet((ahead, me_x)))
    pl.when(leads == 1)(lambda: greet((behind, me_x)))
    expected = expected + 1 - leads + led
    for copy in local:
        copy.start()
    pl.semaphore_wait(barrier, expected)
    for j in answer_order:
        pl.when(me_w >= offs[j] if j > 1 else leads == 0)(
            lambda j=j: pl.semaphore_signal(
                esem.at[j], inc=1, device_id=(me_w - offs[j], me_x), device_id_type=MESH
            )
        )
    tcopies = [
        pltpu.make_async_remote_copy(
            src_ref=tokb.at[me_x], dst_ref=tokb.at[me_x], send_sem=tsend.at[d - 1], recv_sem=trecv.at[d - 1],
            device_id=(me_w, lax.rem(me_x + d, narrow)), device_id_type=MESH,
        )
        for d in range(1, narrow)
    ]
    far_first = sorted(range(1, narrow), key=lambda d: -min(d, narrow - d))
    local[0].wait()
    for d in far_first:
        tcopies[d - 1].start()
    local[2].wait()
    wqb[...] = wqkb[:, 0, :]
    local[1].wait()
    for copy in tcopies:
        copy.wait_recv()

    floats = [tokb[i].astype(jnp.float32) for i in range(narrow)]
    square = functools.reduce(
        jnp.add, [jnp.sum(f * f, axis=-1, keepdims=True) for f in floats]
    )
    scale = lax.rsqrt(square / (narrow * width) + 1e-06)
    normed = [
        (floats[i] * scale * gainb[:, i * width:(i + 1) * width]).astype(jnp.bfloat16)
        for i in range(narrow)
    ]

    def project(weight):
        return functools.reduce(
            jnp.add,
            [
                jnp.dot(
                    normed[i], weight(i * width, (i + 1) * width),
                    preferred_element_type=jnp.float32,
                )
                for i in range(narrow)
            ],
        ).astype(jnp.bfloat16)

    query = project(lambda a, b: wqb[a:b])
    qin[0] = query

    def query_copy(source, o, j):
        return pltpu.make_async_remote_copy(
            src_ref=qin.at[source], dst_ref=qin.at[j], send_sem=qsend.at[j], recv_sem=qrecv.at[j],
            device_id=(lax.rem(me_w + o, wide), me_x), device_id_type=MESH,
        )

    qcopies = {j: query_copy(0, offs[j], j) for j in direct + relayed}
    quarter = wide // 4
    relay = (wide - 1 - me_w) // (2 * quarter)
    back = relay * (1 - me_w // quarter)
    source = 2 + 4 * back
    relays = {
        4: query_copy(source, offs[2] + back * (offs[6] - offs[2]), 4),
        5: query_copy(source, offs[3] + back * (offs[7] - offs[3]), 5),
    }
    relay_odd = (relay > 0) & (me_w != quarter - 1)

    def known(j):
        pl.when(me_w + offs[j] >= wide if j > 1 else led == 1)(qcopies[j].start)

    def unknown(j):
        @pl.when(me_w + offs[j] < wide if j > 1 else led == 0)
        def _():
            pl.semaphore_wait(esem.at[j], 1)
            qcopies[j].start()

    for j in relayed + direct:
        known(j)
    for j in (1, 2, 3):
        unknown(j)

    lane = lax.broadcasted_iota(jnp.int32, (tcount, 128), 1)
    head_of = lax.broadcasted_iota(jnp.int32, (tcount, width), 1) // HEAD_DIM

    def stat_tile(columns, base, start):
        tile = start
        for h, column in enumerate(columns):
            tile = jnp.where(lane == base + h, column, tile)
        return tile

    local[4].wait()
    local[5].wait()
    local[6].wait()
    row = lax.broadcasted_iota(jnp.int32, (tcount, span), 0)
    place = lax.broadcasted_iota(jnp.int32, (tcount, span), 1) - row * page_len

    def offset(j):
        return (j - j % 2) * stride_len + j % 2

    def attend(j):
        home = lax.rem(me_w + (wide - offset(j)), wide) * tcount
        q = qin[j].astype(jnp.float32)
        spread = jnp.concatenate(
            [jnp.where(head_of == h, q, 0.0) for h in range(heads)], axis=0
        ).astype(jnp.bfloat16)
        slots = [ptb[j, home + r] for r in range(tcount)]
        keys = jnp.concatenate([kvb[s, 0] for s in slots], axis=0)
        values = jnp.concatenate([kvb[s, 1] for s in slots], axis=0)
        limit = jnp.full((tcount, span), 0, jnp.int32)
        for r in range(tcount):
            limit = jnp.where(
                row == r, jnp.minimum(lenb[home + r] - j * page_len, page_len), limit
            )
        valid1 = (place >= 0) & (place < limit)
        valid = jnp.concatenate([valid1] * heads, axis=0)
        scores = lax.dot_general(
            spread, keys, (((1,), (1,)), ((), ())), preferred_element_type=jnp.float32
        )
        scores = jnp.where(valid, scores, NEG)
        top = jnp.max(scores, axis=-1, keepdims=True)
        weights = jnp.where(valid, jnp.exp(scores - top), 0.0)
        total = jnp.sum(weights, axis=-1, keepdims=True)
        acc = jnp.dot(weights.astype(jnp.bfloat16), values, preferred_element_type=jnp.float32)
        mine = jnp.zeros((tcount, width), jnp.float32)
        for h in range(heads):
            mine = jnp.where(head_of == h, acc[h * tcount:(h + 1) * tcount], mine)
        stats = stat_tile(
            [top[h * tcount:(h + 1) * tcount] for h in range(heads)],
            0, jnp.full((tcount, 128), 0.0, jnp.float32),
        )
        stats = stat_tile(
            [total[h * tcount:(h + 1) * tcount] for h in range(heads)], 64, stats
        )
        return mine, stats

    def partial_copy(j):
        return pltpu.make_async_remote_copy(
            src_ref=pout.at[j], dst_ref=pin.at[j], send_sem=psend.at[j], recv_sem=precv.at[j],
            device_id=(lax.rem(me_w + (wide - offset(j)), wide), me_x), device_id_type=MESH,
        )

    def keep(ref, j, result):
        high = result[1].astype(jnp.bfloat16).astype(jnp.float32)
        middle = (result[1] - high).astype(jnp.bfloat16).astype(jnp.float32)
        terms = high + pltpu.roll(middle, 16, 1) + pltpu.roll(result[1] - high - middle, 32, 1)
        ref[j, :, :width] = result[0].astype(jnp.bfloat16)
        ref[j, :, width:] = terms.astype(jnp.bfloat16)

    def statistics(j):
        terms = pin[j, :, width:].astype(jnp.float32)
        return terms + (pltpu.roll(terms, 128 - 16, 1) + pltpu.roll(terms, 128 - 32, 1))

    def own_part():
        keep(pin, 0, attend(0))
        new_keys = project(lambda a, b: wqkb[a:b, 1, :]).astype(jnp.float32)
        local[3].wait()
        newb[...] = project(lambda a, b: wvb[a:b, :]).astype(jnp.float32)
        products = query.astype(jnp.float32) * new_keys
        selfb[...] = stat_tile(
            [
                jnp.sum(jnp.where(head_of == h, products, 0.0), axis=-1, keepdims=True)
                for h in range(heads)
            ],
            0, jnp.full((tcount, 128), NEG, jnp.float32),
        )

    part = me_w // quarter
    pl.when(part == 0)(own_part)
    for j in direct[3:]:
        unknown(j)

    @pl.when(relay > 0)
    def _():
        query_copy(0, offs[2], source).wait_recv()
        relays[4].start()
        pl.when(relay_odd)(relays[5].start)

    def digits(order):
        return sum(j * 8**at for at, j in enumerate(order))

    row_first = 1 - (in_row + row_len - 1) // row_len
    part_first = 1 - (lax.rem(me_w, quarter) + quarter - 1) // quarter
    code = 0
    for at, orders in enumerate(ORDERS):
        inside, start, edge = (digits(order) for order in orders)
        here = 1 - (lax.rem(part - at + 4, 4) + 3) // 4
        code = code + here * (inside + row_first * (start - inside) + part_first * (edge - start))

    def page(step, code):
        j = lax.rem(code, 8)
        pl.when((j != source) | (relay == 0))(query_copy(0, offs[2], j).wait_recv)
        keep(pout, j, attend(j))
        partial_copy(j).start()
        return code // 8

    lax.fori_loop(0, pages - 1, page, code)
    pl.when(part > 0)(own_part)
    def widen(tile):
        wide_tile = jnp.zeros((tcount, width), jnp.float32)
        for h in range(heads):
            wide_tile = jnp.where(head_of == h, tile[:, h:h + 1], wide_tile)
        return wide_tile

    def merge(js, best, denom, numer):
        stats = [statistics(j) for j in js]
        higher = functools.reduce(jnp.maximum, stats, best)
        scale = jnp.exp(best - higher)
        denom, numer = scale * denom, widen(scale) * numer
        for j, stat in zip(js, stats):
            factor = jnp.exp(stat - higher)
            denom = denom + factor * pltpu.roll(stat, 64, 1)
            numer = numer + widen(factor) * pin[j, :, :width].astype(jnp.float32)
        return higher, denom, numer

    for j in direct:
        partial_copy(j).wait_recv()
    merged = merge((0,) + direct, selfb[...], jnp.ones((tcount, 128), jnp.float32), newb[...])
    for j in relayed:
        partial_copy(j).wait_recv()
    _, denom, numer = merge(relayed, *merged)
    heads_out = (numer / widen(denom)).astype(jnp.bfloat16)

    local[7].wait()
    rcopies = []
    for d in far_first:
        peer = lax.rem(me_x + d, narrow)
        start = pl.multiple_of(peer * width, width)
        rsout[d - 1] = jnp.dot(
            heads_out, wob[:, pl.ds(start, width)], preferred_element_type=jnp.float32
        )
        copy = pltpu.make_async_remote_copy(
            src_ref=rsout.at[d - 1], dst_ref=out.at[d - 1],
            send_sem=rsend.at[d - 1], recv_sem=rrecv.at[d - 1],
            device_id=(me_w, peer), device_id_type=MESH,
        )
        copy.start()
        rcopies.append(copy)
    start = pl.multiple_of(me_x * width, width)
    rsout[narrow - 1] = jnp.dot(
        heads_out, wob[:, pl.ds(start, width)], preferred_element_type=jnp.float32
    )
    own = pltpu.make_async_copy(rsout.at[narrow - 1], out.at[narrow - 1], lsem.at[0])
    own.start()
    for copy in tcopies + [partial_copy(j) for j in range(1, pages)]:
        copy.wait_send()
    for j in direct:
        qcopies[j].wait_send()
    for j in relayed:
        pl.when(me_w + offs[j] >= wide)(qcopies[j].wait_send)
    pl.when(relay > 0)(relays[4].wait_send)
    pl.when(relay_odd)(relays[5].wait_send)
    own.wait()
    for copy in rcopies:
        copy.wait()


def body(wide, narrow, tokens, norm_gain, w_qk, w_value, w_out, kv_cache, cache_len, page_table):
    tcount, width = tokens.shape
    total, pages = page_table.shape
    features = norm_gain.shape[0]
    stride_len = wide // pages
    anywhere = pl.BlockSpec(memory_space=pltpu.HBM)
    dma = pltpu.SemaphoreType.DMA
    sums = pl.pallas_call(
        functools.partial(layer_kernel, wide, narrow, stride_len, wide // 16),
        out_shape=jax.ShapeDtypeStruct((narrow, tcount, width), jnp.float32),
        in_specs=[anywhere] * 8,
        out_specs=pl.BlockSpec(memory_space=pl.ANY),
        scratch_shapes=[
            pltpu.VMEM((narrow, tcount, width), jnp.bfloat16),
            pltpu.VMEM((1, features), jnp.float32),
            pltpu.VMEM(w_qk.shape, jnp.bfloat16),
            pltpu.VMEM((features, width), jnp.bfloat16),
            pltpu.VMEM(w_value.shape, jnp.bfloat16),
            pltpu.VMEM(w_out.shape, jnp.bfloat16),
            pltpu.VMEM(kv_cache.shape, jnp.bfloat16),
            pltpu.SMEM((total,), jnp.int32),
            pltpu.SMEM((pages, total), jnp.int32),
            pltpu.VMEM((pages, tcount, width), jnp.bfloat16),
            pltpu.VMEM((pages, tcount, width + 128), jnp.bfloat16),
            pltpu.VMEM((pages, tcount, width + 128), jnp.bfloat16),
            pltpu.VMEM((narrow, tcount, width), jnp.float32),
            dma((8,)),
            dma((narrow - 1,)), dma((narrow - 1,)),
            dma((pages,)), dma((pages,)),
            dma((pages,)), dma((pages,)),
            dma((narrow - 1,)), dma((narrow - 1,)),
            pltpu.SemaphoreType.REGULAR((pages,)),
            pltpu.VMEM((tcount, width), jnp.float32),
            pltpu.VMEM((tcount, 128), jnp.float32),
        ],
        compiler_params=pltpu.CompilerParams(
            collective_id=0, has_side_effects=True, vmem_limit_bytes=62 << 20
        ),
    )(
        tokens, norm_gain.reshape(1, features), w_qk, w_value, w_out, kv_cache, cache_len,
        page_table.T,
    )
    return jnp.sum(sums, axis=0).astype(jnp.bfloat16)


def solution(mesh):
    placed = (
        P("wide", "narrow"),
        P(),
        P(None, None, "narrow"),
        P(None, "narrow"),
        P("narrow", None),
        P("wide", None, None, "narrow"),
        P(),
        P(),
    )
    return jax.shard_map(
        functools.partial(body, mesh.shape["wide"], mesh.shape["narrow"]),
        mesh=mesh, in_specs=placed, out_specs=P("wide", "narrow"), check_vma=False,
    )
```
